512 devices in a mesh: tm: 256 (over z, y, x), space: 2 (over core).
Axes of the slice: x: 4, y: 8, z: 8, core: 2. Of those that a mesh axis runs over, the one named last changes fastest.
Arguments:
- image_gradient: bfloat16 [512, 128, 3, 4096], P('tm', 'space'), may hold values from -0.375 to 0.375
- residual: bfloat16 [512, 128, 4096], P('tm', 'space'), may hold values from -6 to 6
- phase: float32 [512], P('tm'), may hold values from 0 to 1
- counts: int32 [128], P('space'), may hold values from 512 to 4096
- owner: int32 [128, 1], P('space'), may hold values from 0 to 1, as said below
Outputs:
- hessian_blocks: float32 [512, 192, 576], P('tm', 'space')
- gradient_blocks: float32 [512, 192, 24], P('tm', 'space')
The draws below stay inside these ranges and needn't reach their ends.
Inputs may be any that keep to these rules, and one draw needn't show every extreme that they name: Among the 64 bricks of each aligned block at most 48 share an owner, and one owner takes exactly 48 bricks of every block.
All inputs are finite; a program needn't handle non-finite values.
Results may differ from the reference program's by a relative error of at most 0.0029.
Values sent between devices are 32-bit elements; how exact they have to be, the bound alone decides.
A program may use at most 64 MiB of HBM per device.

```python
import jax
import jax.numpy as jnp
from jax import lax

EDGE = 16
VOX = 4096
SPD = 24
BR = 64
STEPS = 512
BRICKS = 128
CAP = 48
SLOTS = 192
N_SPACE = 2


def draw_image_gradient(key, part):
    shape = (STEPS, BRICKS, 3, VOX)
    common_shape = (STEPS, BRICKS, 1, VOX)
    lone_entry = jnp.clip(jax.random.normal(jax.random.fold_in(key, 31), shape, jnp.float32), -4.0, 4.0)
    common_across = jnp.clip(jax.random.normal(jax.random.fold_in(key, 32), common_shape, jnp.float32), -4.0, 4.0)
    return ((lone_entry + common_across) * 3.0 * VOX ** (-0.5)).astype(jnp.bfloat16)


def draw_owner(key, part):
    owners = BRICKS // BR
    label_count = owners * CAP
    labels = jnp.arange(label_count, dtype=jnp.int32) // CAP
    busiest = jax.random.randint(jax.random.fold_in(key, 7), (), 0, owners)

    def one_block(block):
        block_key = jax.random.fold_in(jax.random.fold_in(key, 13), block)
        order_first = jax.random.permutation(block_key, label_count)
        picked = labels[order_first]
        spots = jnp.arange(label_count, dtype=jnp.int32)
        priority = jnp.where(picked == busiest, spots, label_count + spots)
        chosen = picked[jnp.argsort(priority, stable=True)][:BR]
        return chosen[jax.random.permutation(jax.random.fold_in(block_key, 1), BR)]
    return jax.vmap(one_block)(jnp.arange(owners, dtype=jnp.int32)).reshape(BRICKS, 1).astype(jnp.int32)


def with_ends(array, stream_key, least, largest):
    spot = [jax.random.randint(jax.random.fold_in(stream_key, axis), (), 0, length) for axis, length in enumerate(array.shape)]
    main_axis = array.shape.index(max(array.shape))
    beside = spot[:main_axis] + [(spot[main_axis] + 1) % array.shape[main_axis]] + spot[main_axis + 1:]
    return array.at[tuple(spot)].set(least).at[tuple(beside)].set(largest)


def shard_levels(rng, shape, split, low, largest):
    def one(axis_at, blocks):
        heights = jax.random.uniform(jax.random.fold_in(jax.random.fold_in(rng, 6), axis_at), (blocks,), jnp.float32, low / len(split), largest / len(split))
        return jnp.repeat(jnp.exp(heights), shape[axis_at] // blocks).reshape((-1,) + (1,) * (len(shape) - axis_at - 1))

    factor_of = one(*split[0])
    for cut in split[1:]:
        factor_of = factor_of * one(*cut)
    return factor_of


def centred(stream_key, dims, scale, reach, cuts=(), held_as=jnp.bfloat16):
    factor_of = shard_levels(stream_key, dims, cuts, -0.22, 0.18) if cuts else 1.0
    entries = jax.random.normal(stream_key, dims, jnp.float32) * scale * factor_of
    return jnp.minimum(jnp.maximum(entries, -reach), reach).astype(held_as)


def setup_inputs(seed: int = 0) -> dict:
    key_list = jax.random.split(jax.random.key(seed), 6)
    return {
        "image_gradient": draw_image_gradient(jax.random.fold_in(key_list[5], 71), 0),
        "residual": centred(key_list[1], (STEPS, BRICKS, VOX), 1.0, 6.0, ((0, 256), (1, 2))),
        "phase": jnp.clip(1.0 * jax.random.uniform(key_list[2], (STEPS,), jnp.float32) ** shard_levels(key_list[2], (STEPS,), ((0, 256),), -0.2, 0.2), 0.0, 1.0),
        "counts": with_ends(jax.random.randint(key_list[3], (BRICKS,), VOX // 8, VOX + 1), jax.random.fold_in(key_list[3], 1), VOX // 8, VOX).astype(jnp.int32),
        "owner": draw_owner(jax.random.fold_in(key_list[5], 71), 0),
    }


def spline_weights(phase):
    u = phase.astype(jnp.float32)
    return jnp.stack([(1.0 - u) ** 3 / 6.0, (3.0 * u ** 3 - 6.0 * u ** 2 + 4.0) / 6.0,
                      (-3.0 * u ** 3 + 3.0 * u ** 2 + 3.0 * u + 1.0) / 6.0, u ** 3 / 6.0], axis=-1)


def shape_table(edge):
    voxel = jnp.arange(edge * edge * edge, dtype=jnp.int32)
    first = ((voxel // (edge * edge)).astype(jnp.float32) + 0.5) / edge
    second = (((voxel // edge) % edge).astype(jnp.float32) + 0.5) / edge
    third = ((voxel % edge).astype(jnp.float32) + 0.5) / edge
    rows = []
    for node in range(8):
        along_first = first if (node >> 2) & 1 else 1.0 - first
        along_second = second if (node >> 1) & 1 else 1.0 - second
        along_third = third if node & 1 else 1.0 - third
        rows.append(along_first * along_second * along_third)
    return jnp.stack(rows, axis=0)


def reference(image_gradient, residual, phase, counts, owner):
    valid_mask = lax.broadcasted_iota(jnp.int32, (BRICKS, VOX), 1) < counts[:, None]
    shapes = shape_table(EDGE)

    def per_step(pair):
        grads, resid = pair
        product = shapes[None, :, None, :] * grads.astype(jnp.float32)[:, None, :, :]
        sens = product.reshape(BRICKS, SPD, VOX).astype(jnp.bfloat16)
        masked = jnp.where(valid_mask[:, None, :], sens, jnp.zeros((), jnp.bfloat16))
        wide = masked.astype(jnp.float32)
        hessian = jnp.einsum("bdv,bev->bde", wide, wide, precision=lax.Precision.HIGHEST).reshape(BRICKS, SPD * SPD)
        gradient = jnp.einsum("bdv,bv->bd", wide, resid.astype(jnp.float32), precision=lax.Precision.HIGHEST)
        return hessian, gradient

    step_hessian, step_gradient = lax.map(per_step, (image_gradient, residual))
    weights = spline_weights(phase)
    target = jnp.clip(jnp.arange(STEPS, dtype=jnp.int32)[:, None] - 1 + jnp.arange(4, dtype=jnp.int32)[None, :], 0, STEPS - 1)
    hits_table = (target[:, :, None] == jnp.arange(STEPS, dtype=jnp.int32)[None, None, :]).astype(jnp.float32)
    basis_lookup_grid = jnp.einsum("tj,tjk->tk", weights, hits_table, precision=lax.Precision.HIGHEST)
    coef_hessian = jnp.einsum("tk,tbf->kbf", basis_lookup_grid * basis_lookup_grid, step_hessian, precision=lax.Precision.HIGHEST)
    coef_gradient = jnp.einsum("tk,tbf->kbf", basis_lookup_grid, step_gradient, precision=lax.Precision.HIGHEST)
    owner_flat = owner[:, 0].astype(jnp.int32)
    block_owner = owner_flat.reshape(N_SPACE, BR)
    owner_hits = (block_owner[:, :, None] == jnp.arange(N_SPACE, dtype=jnp.int32)[None, None, :]).astype(jnp.int32)
    earlier = jnp.cumsum(owner_hits, axis=1) - owner_hits
    brick_rank = jnp.sum(earlier * owner_hits, axis=2).reshape(BRICKS).astype(jnp.int32)
    source = (jnp.arange(BRICKS, dtype=jnp.int32) // BR).astype(jnp.int32)
    slot_index = owner_flat * (N_SPACE * CAP) + source * CAP + brick_rank
    hessian_blocks = jnp.zeros((STEPS, SLOTS, SPD * SPD), jnp.float32).at[:, slot_index].set(coef_hessian)
    gradient_blocks = jnp.zeros((STEPS, SLOTS, SPD), jnp.float32).at[:, slot_index].set(coef_gradient)
    return hessian_blocks, gradient_blocks
```

```python
import functools

import jax
import jax.numpy as jnp
import numpy as np
from jax import lax
from jax.experimental import pallas as pl
from jax.experimental.pallas import tpu as pltpu
from jax.sharding import PartitionSpec as P

EDGE = 16
COMPS = 3
NODES = 8
DOFS = NODES * COMPS
PATCH = DOFS * DOFS
MOMENTS = 27
PAIRS = ((0, 0), (0, 1), (0, 2), (1, 1), (1, 2), (2, 2))
ROWS = 80
LANES = 256
GRAD_LANE = 32 * len(PAIRS)
CHUNK = 1024
MESH = pl.DeviceIdType.MESH
F32 = jnp.float32
BF16 = jnp.bfloat16


def two_terms(table):
    high = table.astype(BF16)
    return high, (table - high.astype(np.float64)).astype(BF16)


def moment_table():
    voxel = np.arange(EDGE**3)
    axes = [voxel // (EDGE * EDGE), voxel // EDGE % EDGE, voxel % EDGE]
    u = [(axis + 0.5) / EDGE for axis in axes]
    quads = [((1 - x) ** 2, x * (1 - x), x * x) for x in u]
    lines = [(1 - x, x) for x in u]
    moments = np.stack([quads[0][m // 9] * quads[1][m // 3 % 3] * quads[2][m % 3] for m in range(MOMENTS)])
    shapes = np.stack([lines[0][a >> 2 & 1] * lines[1][a >> 1 & 1] * lines[2][a & 1] for a in range(NODES)])
    table = np.zeros((ROWS, EDGE**3), BF16)
    table[0:MOMENTS], table[32 : 32 + MOMENTS] = two_terms(moments)
    table[64:72], table[72:80] = two_terms(shapes)
    return table


def spread_tables():
    hessian = np.zeros((LANES, PATCH), np.float32)
    gradient = np.zeros((DOFS, LANES), np.float32)
    for a in range(NODES):
        for c in range(COMPS):
            gradient[COMPS * a + c, GRAD_LANE + NODES * c + a] = 1.0
            for b in range(NODES):
                for e in range(COMPS):
                    pair = PAIRS.index((min(c, e), max(c, e)))
                    bits = [(a >> s & 1) + (b >> s & 1) for s in (2, 1, 0)]
                    moment = bits[0] * 9 + bits[1] * 3 + bits[2]
                    hessian[32 * pair + moment, (COMPS * a + c) * DOFS + COMPS * b + e] = 1.0
    return hessian.astype(BF16), gradient.astype(BF16)


def split3(x):
    first = x.astype(BF16)
    rest = x - first.astype(F32)
    second = rest.astype(BF16)
    return first, second, (rest - second.astype(F32)).astype(BF16)


def dot_nt(a, b):
    return lax.dot_general(a, b, (((1,), (1,)), ((), ())), preferred_element_type=F32)


def kernel(
    n,
    image_hbm,
    resid_hbm,
    phase_hbm,
    counts_hbm,
    owner_hbm,
    table_hbm,
    spread_hbm,
    pick_hbm,
    hess_ref,
    grad_ref,
    image,
    resid,
    phase,
    counts,
    owner,
    table,
    spread,
    pick,
    mask,
    acc,
    send_fwd,
    send_back,
    send_side,
    recv_fwd,
    recv_back,
    mine,
    load_sem,
    small_sem,
    fwd_send_sem,
    fwd_recv_sem,
    back_send_sem,
    back_recv_sem,
    side_sem,
):
    bricks, voxels = resid.shape[1], resid.shape[2]
    cap = mine.shape[2]
    chunks = voxels // CHUNK
    d = lax.axis_index("tm")
    s = lax.axis_index("space")
    has_before = d > 0
    has_after = d < n - 1

    small = [
        pltpu.make_async_copy(counts_hbm, counts, small_sem.at[0]),
        pltpu.make_async_copy(owner_hbm, owner, small_sem.at[1]),
        pltpu.make_async_copy(phase_hbm, phase, small_sem.at[2]),
        pltpu.make_async_copy(spread_hbm, spread, small_sem.at[3]),
        pltpu.make_async_copy(pick_hbm, pick, small_sem.at[4]),
    ]
    small[0].start()
    loads = {}
    for t in (1, 0):
        for k in range(chunks):
            span = pl.ds(k * CHUNK, CHUNK)
            loads[t, k] = [
                pltpu.make_async_copy(
                    image_hbm.at[t, :, :, span], image.at[t, :, :, span], load_sem.at[0, t, k]
                ),
                pltpu.make_async_copy(
                    resid_hbm.at[t, :, span], resid.at[t, :, span], load_sem.at[1, t, k]
                ),
            ]
            if t == 1:
                loads[t, k].append(
                    pltpu.make_async_copy(
                        table_hbm.at[:, span], table.at[:, span], load_sem.at[2, t, k]
                    )
                )
            for copy in loads[t, k]:
                copy.start()
    for copy in small[1:]:
        copy.start()

    barrier = pltpu.get_barrier_semaphore()

    def greet(where):
        pl.semaphore_signal(barrier, inc=1, device_id=where, device_id_type=MESH)

    greet((d, 1 - s))

    @pl.when(has_before)
    def _():
        greet((d - 1, 0))
        greet((d - 1, 1))

    @pl.when(has_after)
    def _():
        greet((d + 1, 0))
        greet((d + 1, 1))

    small[0].wait()
    square = lax.broadcasted_iota(jnp.int32, (bricks, bricks), 0) == lax.broadcasted_iota(
        jnp.int32, (bricks, bricks), 1
    )
    count_column = jnp.sum(
        jnp.where(square, jnp.broadcast_to(counts[...].astype(F32), (bricks, bricks)), 0.0),
        axis=1,
        keepdims=True,
    )
    for k in range(voxels // 512):
        voxel = (lax.broadcasted_iota(jnp.int32, (bricks, 512), 1) + k * 512).astype(F32)
        mask[:, k * 512 : (k + 1) * 512] = jnp.where(voxel < count_column, 1.0, 0.0).astype(BF16)

    def step_sums(t):
        for k in range(chunks):
            span = slice(k * CHUNK, (k + 1) * CHUNK)
            for copy in loads[t, k]:
                copy.wait()
            valid = mask[:, span]
            g = [image[t, c, :, span] * valid for c in range(COMPS)]
            r = resid[t, :, span]
            products = [g[c] * g[e] for c, e in PAIRS] + [g[c] * r for c in range(COMPS)]
            part = dot_nt(table[:, span], jnp.concatenate(products, axis=0))
            if k == 0:
                acc[...] = part
            else:
                acc[...] += part
        pairs = len(PAIRS) * bricks
        hess = acc[0:32, :pairs] + acc[32:64, :pairs]
        grad = acc[64:72, pairs:] + acc[72:80, pairs:]
        grad = jnp.concatenate([grad, jnp.zeros((8, bricks), F32)], axis=1)
        rows = []
        for q in range(len(PAIRS)):
            two = hess[:, 128 * (q // 2) : 128 * (q // 2) + 128]
            rows.append(pltpu.roll(two, 64, 1) if q % 2 else two)
        for c in range(COMPS):
            two = grad[:, 128 * (c // 2) : 128 * (c // 2) + 128]
            rows.append(pltpu.roll(two, 64, 1) if c % 2 else two)
        rows.append(jnp.zeros((LANES - GRAD_LANE - 24, 128), F32))
        return jnp.concatenate(rows, axis=0)

    sums = step_sums(1)

    for copy in small[1:3]:
        copy.wait()
    who = jnp.broadcast_to(owner[...].astype(F32), (8, bricks))
    earlier = lax.broadcasted_iota(jnp.int32, (bricks, bricks), 0) < lax.broadcasted_iota(
        jnp.int32, (bricks, bricks), 1
    )
    ones_before = jnp.dot(
        who.astype(BF16), jnp.where(earlier, 1.0, 0.0).astype(BF16), preferred_element_type=F32
    )
    place = lax.broadcasted_iota(jnp.int32, (8, bricks), 1).astype(F32)
    rank = jnp.where(who > 0.5, ones_before, place - ones_before)
    mine_first = jnp.where(s == 0, who, 1.0 - who)
    target = (mine_first * cap + rank)[0:1, :]
    slot = lax.broadcasted_iota(jnp.int32, (2 * cap, bricks), 0).astype(F32)
    hit = jnp.where(slot == jnp.broadcast_to(target, (2 * cap, bricks)), 1.0, 0.0)
    hit = jnp.concatenate([hit, jnp.zeros((2 * cap, 128 - bricks), F32)], axis=1).astype(BF16)

    def placed(x):
        a, b, c = split3(x)
        return dot_nt(hit, a) + dot_nt(hit, b) + dot_nt(hit, c)

    first = jnp.where(has_before, 0.0, 1.0)
    last = jnp.where(has_after, 0.0, 1.0)

    def weights(t):
        u = phase[t]
        v = 1.0 - u
        return (
            v * v * v * (1.0 / 6.0),
            (3.0 * u * u * u - 6.0 * u * u + 4.0) * (1.0 / 6.0),
            (-3.0 * u * u * u + 3.0 * u * u + 3.0 * u + 1.0) * (1.0 / 6.0),
            u * u * u * (1.0 / 6.0),
        )

    w = weights(0)
    basis0 = (w[0] * (1.0 - first), w[1] + first * w[0], w[2] + last * w[3], w[3] * (1.0 - last))
    w = weights(1)
    basis1 = (w[0], w[1] + last * (w[2] + w[3]), w[2] * (1.0 - last), w[3] * (1.0 - last))
    is_hess = lax.broadcasted_iota(jnp.int32, (1, LANES), 1) < GRAD_LANE

    def scale(b):
        return jnp.where(is_hess, b * b, b)

    def remote(src, dst, send_sem, recv_sem, where):
        return pltpu.make_async_remote_copy(
            src_ref=src,
            dst_ref=dst,
            send_sem=send_sem,
            recv_sem=recv_sem,
            device_id=where,
            device_id_type=MESH,
        )

    cores = (s, 1 - s)

    def to_after(k, i):
        return remote(
            send_fwd.at[k, i],
            recv_fwd.at[k, s],
            fwd_send_sem.at[k, i],
            fwd_recv_sem.at[k, s],
            (d + 1, cores[i]),
        )

    def to_before(i):
        return remote(
            send_back.at[i],
            recv_back.at[s],
            back_send_sem.at[i],
            back_recv_sem.at[s],
            (d - 1, cores[i]),
        )

    side = remote(send_side, mine.at[s], side_sem.at[0], side_sem.at[1], (d, 1 - s))

    placed1 = placed(sums)
    ahead = placed1 * scale(basis1[3])
    for i in range(2):
        send_fwd[1, i] = ahead[i * cap : (i + 1) * cap]

    pl.semaphore_wait(barrier, 1 + 2 * has_before.astype(jnp.int32) + 2 * has_after.astype(jnp.int32))

    @pl.when(jnp.logical_not(has_before))
    def _():
        recv_fwd[...] = jnp.zeros(recv_fwd.shape, F32)

    @pl.when(has_after)
    def _():
        for i in range(2):
            to_after(1, i).start()

    @pl.when(jnp.logical_not(has_after))
    def _():
        recv_back[...] = jnp.zeros(recv_back.shape, F32)

    sums = step_sums(0)
    placed0 = placed(sums)
    ahead = placed0 * scale(basis0[3]) + placed1 * scale(basis1[2])
    behind = placed0 * scale(basis0[0])
    for i in range(2):
        send_fwd[0, i] = ahead[i * cap : (i + 1) * cap]
        send_back[i] = behind[i * cap : (i + 1) * cap]

    @pl.when(has_after)
    def _():
        for i in range(2):
            to_after(0, i).start()

    @pl.when(has_before)
    def _():
        for i in range(2):
            to_before(i).start()

    for k in range(2):
        own = placed0 * scale(basis0[1 + k]) + placed1 * scale(basis1[k])
        mine[s, k] = own[:cap]
        send_side[k] = own[cap:]
    side.start()

    for copy in small[3:]:
        copy.wait()
    side.wait_send()
    remote(send_side, mine.at[1 - s], side_sem.at[0], side_sem.at[1], (d, 1 - s)).wait_recv()

    @pl.when(has_after)
    def _():
        for i in range(2):
            to_after(1, i).wait_send()
            to_after(0, i).wait_send()
            remote(
                send_back.at[i],
                recv_back.at[i],
                back_send_sem.at[i],
                back_recv_sem.at[i],
                (d + 1, i),
            ).wait_recv()

    @pl.when(has_before)
    def _():
        for i in range(2):
            to_before(i).wait_send()
            for k in range(2):
                remote(
                    send_fwd.at[k, i],
                    recv_fwd.at[k, i],
                    fwd_send_sem.at[k, i],
                    fwd_recv_sem.at[k, i],
                    (d - 1, i),
                ).wait_recv()

    for k in range(2):
        total = [mine[i, k] + recv_fwd[k, i] for i in range(2)]
        if k == 1:
            total = [total[i] + recv_back[i] for i in range(2)]
        parts = split3(jnp.concatenate(total, axis=0))
        table_h = spread[...]
        hess_ref[k] = sum(jnp.dot(part, table_h, preferred_element_type=F32) for part in parts)
        grad_ref[k] = sum(dot_nt(pick[...], part) for part in parts)


def per_device(n, n_space, image_gradient, residual, phase, counts, owner):
    steps, bricks, comps, voxels = image_gradient.shape
    cap = 3 * bricks // (2 * n_space)
    slots = n_space * cap
    hessian_lanes, gradient_lanes = spread_tables()
    hbm = pl.BlockSpec(memory_space=pltpu.HBM)
    vmem = pl.BlockSpec(memory_space=pltpu.VMEM)
    chunks = voxels // CHUNK
    dma = pltpu.SemaphoreType.DMA
    hess, grad = pl.pallas_call(
        functools.partial(kernel, n),
        out_shape=(
            jax.ShapeDtypeStruct((steps, slots, PATCH), F32),
            jax.ShapeDtypeStruct((steps, DOFS, slots), F32),
        ),
        in_specs=[hbm] * 8,
        out_specs=(vmem, vmem),
        scratch_shapes=[
            pltpu.VMEM((steps, comps, bricks, voxels), BF16),
            pltpu.VMEM((steps, bricks, voxels), BF16),
            pltpu.SMEM((steps,), F32),
            pltpu.VMEM((1, bricks), jnp.int32),
            pltpu.VMEM((1, bricks), jnp.int32),
            pltpu.VMEM((ROWS, voxels), BF16),
            pltpu.VMEM((LANES, PATCH), BF16),
            pltpu.VMEM((DOFS, LANES), BF16),
            pltpu.VMEM((bricks, voxels), BF16),
            pltpu.VMEM((ROWS, 9 * bricks), F32),
            pltpu.VMEM((2, 2, cap, LANES), F32),
            pltpu.VMEM((2, cap, LANES), F32),
            pltpu.VMEM((2, cap, LANES), F32),
            pltpu.VMEM((2, 2, cap, LANES), F32),
            pltpu.VMEM((2, cap, LANES), F32),
            pltpu.VMEM((2, 2, cap, LANES), F32),
            dma((3, 2, chunks)),
            dma((5,)),
            dma((2, 2)),
            dma((2, 2)),
            dma((2,)),
            dma((2,)),
            dma((2,)),
        ],
        compiler_params=pltpu.CompilerParams(
            collective_id=0, has_side_effects=True, vmem_limit_bytes=48 << 20
        ),
    )(
        jnp.transpose(image_gradient, (0, 2, 1, 3)),
        residual,
        phase,
        counts.reshape(1, bricks),
        owner.reshape(1, bricks),
        moment_table(),
        hessian_lanes,
        gradient_lanes,
    )
    return hess, jnp.transpose(grad, (0, 2, 1))


def solution(mesh):
    in_specs = (
        P("tm", "space", None, None),
        P("tm", "space", None),
        P("tm"),
        P("space"),
        P("space", None),
    )
    out_specs = (P("tm", "space", None), P("tm", "space", None))
    return jax.shard_map(
        functools.partial(per_device, mesh.shape["tm"], mesh.shape["space"]),
        mesh=mesh,
        in_specs=in_specs,
        out_specs=out_specs,
        check_vma=False,
    )
```

```python
import functools

import jax
import jax.numpy as jnp
import numpy as np
from jax import lax
from jax.experimental import pallas as pl
from jax.experimental.pallas import tpu as pltpu
from jax.sharding import PartitionSpec as P

EDGE = 16
COMPS = 3
NODES = 8
DOFS = NODES * COMPS
PATCH = DOFS * DOFS
MOMENTS = 27
PAIRS = ((0, 0), (0, 1), (0, 2), (1, 1), (1, 2), (2, 2))
ROWS = 80
LANES = 256
GRAD_LANE = 32 * len(PAIRS)
CHUNK = 1024
MESH = pl.DeviceIdType.MESH
F32 = jnp.float32
BF16 = jnp.bfloat16


def two_terms(table):
    high = table.astype(BF16)
    return high, (table - high.astype(np.float64)).astype(BF16)


def moment_table():
    voxel = np.arange(EDGE**3)
    axes = [voxel // (EDGE * EDGE), voxel // EDGE % EDGE, voxel % EDGE]
    u = [(axis + 0.5) / EDGE for axis in axes]
    quads = [((1 - x) ** 2, x * (1 - x), x * x) for x in u]
    lines = [(1 - x, x) for x in u]
    moments = np.stack([quads[0][m // 9] * quads[1][m // 3 % 3] * quads[2][m % 3] for m in range(MOMENTS)])
    shapes = np.stack([lines[0][a >> 2 & 1] * lines[1][a >> 1 & 1] * lines[2][a & 1] for a in range(NODES)])
    table = np.zeros((ROWS, EDGE**3), BF16)
    table[0:MOMENTS], table[32 : 32 + MOMENTS] = two_terms(moments)
    table[64:72], table[72:80] = two_terms(shapes)
    return table


def spread_tables():
    hessian = np.zeros((LANES, PATCH), np.float32)
    gradient = np.zeros((DOFS, LANES), np.float32)
    for a in range(NODES):
        for c in range(COMPS):
            gradient[COMPS * a + c, GRAD_LANE + NODES * c + a] = 1.0
            for b in range(NODES):
                for e in range(COMPS):
                    pair = PAIRS.index((min(c, e), max(c, e)))
                    bits = [(a >> s & 1) + (b >> s & 1) for s in (2, 1, 0)]
                    moment = bits[0] * 9 + bits[1] * 3 + bits[2]
                    hessian[32 * pair + moment, (COMPS * a + c) * DOFS + COMPS * b + e] = 1.0
    return hessian.astype(BF16), gradient.astype(BF16)


def split3(x):
    first = x.astype(BF16)
    rest = x - first.astype(F32)
    second = rest.astype(BF16)
    return first, second, (rest - second.astype(F32)).astype(BF16)


def dot_nt(a, b):
    return lax.dot_general(a, b, (((1,), (1,)), ((), ())), preferred_element_type=F32)


def kernel(
    n,
    image_hbm,
    resid_hbm,
    phase_hbm,
    counts_hbm,
    owner_hbm,
    table_hbm,
    spread_hbm,
    pick_hbm,
    hess_ref,
    grad_ref,
    image,
    resid,
    phase,
    counts,
    owner,
    table,
    spread,
    pick,
    mask,
    acc,
    send_fwd,
    send_back,
    send_side,
    recv_fwd,
    recv_back,
    mine,
    load_sem,
    small_sem,
    fwd_send_sem,
    fwd_recv_sem,
    back_send_sem,
    back_recv_sem,
    side_sem,
):
    bricks, voxels = resid.shape[1], resid.shape[2]
    cap = mine.shape[2]
    chunks = voxels // CHUNK
    d = lax.axis_index("tm")
    s = lax.axis_index("space")
    has_before = d > 0
    has_after = d < n - 1

    small = [
        pltpu.make_async_copy(counts_hbm, counts, small_sem.at[0]),
        pltpu.make_async_copy(owner_hbm, owner, small_sem.at[1]),
        pltpu.make_async_copy(phase_hbm, phase, small_sem.at[2]),
        pltpu.make_async_copy(spread_hbm, spread, small_sem.at[3]),
        pltpu.make_async_copy(pick_hbm, pick, small_sem.at[4]),
    ]
    small[0].start()
    loads = {}
    for t in (1, 0):
        for k in range(chunks):
            span = pl.ds(k * CHUNK, CHUNK)
            loads[t, k] = [
                pltpu.make_async_copy(
                    image_hbm.at[t, :, :, span], image.at[t, :, :, span], load_sem.at[0, t, k]
                ),
                pltpu.make_async_copy(
                    resid_hbm.at[t, :, span], resid.at[t, :, span], load_sem.at[1, t, k]
                ),
            ]
            if t == 1:
                loads[t, k].append(
                    pltpu.make_async_copy(
                        table_hbm.at[:, span], table.at[:, span], load_sem.at[2, t, k]
                    )
                )
            for copy in loads[t, k]:
                copy.start()
    for copy in small[1:]:
        copy.start()

    barrier = pltpu.get_barrier_semaphore()

    def greet(where):
        pl.semaphore_signal(barrier, inc=1, device_id=where, device_id_type=MESH)

    greet((d, 1 - s))

    @pl.when(has_before)
    def _():
        greet((d - 1, 0))
        greet((d - 1, 1))

    @pl.when(has_after)
    def _():
        greet((d + 1, 0))
        greet((d + 1, 1))

    small[0].wait()
    square = lax.broadcasted_iota(jnp.int32, (bricks, bricks), 0) == lax.broadcasted_iota(
        jnp.int32, (bricks, bricks), 1
    )
    count_column = jnp.sum(
        jnp.where(square, jnp.broadcast_to(counts[...].astype(F32), (bricks, bricks)), 0.0),
        axis=1,
        keepdims=True,
    )
    for k in range(voxels // 512):
        voxel = (lax.broadcasted_iota(jnp.int32, (bricks, 512), 1) + k * 512).astype(F32)
        mask[:, k * 512 : (k + 1) * 512] = jnp.where(voxel < count_column, 1.0, 0.0).astype(BF16)

    def step_sums(t):
        for k in range(chunks):
            span = slice(k * CHUNK, (k + 1) * CHUNK)
            for copy in loads[t, k]:
                copy.wait()
            valid = mask[:, span]
            g = [image[t, c, :, span] * valid for c in range(COMPS)]
            r = resid[t, :, span]
            products = [g[c] * g[e] for c, e in PAIRS] + [g[c] * r for c in range(COMPS)]
            part = dot_nt(table[:, span], jnp.concatenate(products, axis=0))
            if k == 0:
                acc[...] = part
            else:
                acc[...] += part
        pairs = len(PAIRS) * bricks
        hess = acc[0:32, :pairs] + acc[32:64, :pairs]
        grad = acc[64:72, pairs:] + acc[72:80, pairs:]
        grad = jnp.concatenate([grad, jnp.zeros((8, bricks), F32)], axis=1)
        rows = []
        for q in range(len(PAIRS)):
            two = hess[:, 128 * (q // 2) : 128 * (q // 2) + 128]
            rows.append(pltpu.roll(two, 64, 1) if q % 2 else two)
        for c in range(COMPS):
            two = grad[:, 128 * (c // 2) : 128 * (c // 2) + 128]
            rows.append(pltpu.roll(two, 64, 1) if c % 2 else two)
        rows.append(jnp.zeros((LANES - GRAD_LANE - 24, 128), F32))
        return jnp.concatenate(rows, axis=0)

    sums = step_sums(1)

    for copy in small[1:3]:
        copy.wait()
    who = jnp.broadcast_to(owner[...].astype(F32), (8, bricks))
    earlier = lax.broadcasted_iota(jnp.int32, (bricks, bricks), 0) < lax.broadcasted_iota(
        jnp.int32, (bricks, bricks), 1
    )
    ones_before = jnp.dot(
        who.astype(BF16), jnp.where(earlier, 1.0, 0.0).astype(BF16), preferred_element_type=F32
    )
    place = lax.broadcasted_iota(jnp.int32, (8, bricks), 1).astype(F32)
    rank = jnp.where(who > 0.5, ones_before, place - ones_before)
    mine_first = jnp.where(s == 0, who, 1.0 - who)
    target = (mine_first * cap + rank)[0:1, :]
    slot = lax.broadcasted_iota(jnp.int32, (2 * cap, bricks), 0).astype(F32)
    hit = jnp.where(slot == jnp.broadcast_to(target, (2 * cap, bricks)), 1.0, 0.0)
    hit = jnp.concatenate([hit, jnp.zeros((2 * cap, 128 - bricks), F32)], axis=1).astype(BF16)

    def placed(x):
        a, b, c = split3(x)
        return dot_nt(hit, a) + dot_nt(hit, b) + dot_nt(hit, c)

    first = jnp.where(has_before, 0.0, 1.0)
    last = jnp.where(has_after, 0.0, 1.0)

    def weights(t):
        u = phase[t]
        v = 1.0 - u
        return (
            v * v * v * (1.0 / 6.0),
            (3.0 * u * u * u - 6.0 * u * u + 4.0) * (1.0 / 6.0),
            (-3.0 * u * u * u + 3.0 * u * u + 3.0 * u + 1.0) * (1.0 / 6.0),
            u * u * u * (1.0 / 6.0),
        )

    w = weights(0)
    basis0 = (w[0] * (1.0 - first), w[1] + first * w[0], w[2] + last * w[3], w[3] * (1.0 - last))
    w = weights(1)
    basis1 = (w[0], w[1] + last * (w[2] + w[3]), w[2] * (1.0 - last), w[3] * (1.0 - last))
    is_hess = lax.broadcasted_iota(jnp.int32, (1, LANES), 1) < GRAD_LANE

    def scale(b):
        return jnp.where(is_hess, b * b, b)

    def remote(src, dst, send_sem, recv_sem, where):
        return pltpu.make_async_remote_copy(
            src_ref=src,
            dst_ref=dst,
            send_sem=send_sem,
            recv_sem=recv_sem,
            device_id=where,
            device_id_type=MESH,
        )

    cores = (s, 1 - s)

    def to_after(k, i):
        return remote(
            send_fwd.at[k, i],
            recv_fwd.at[k, s],
            fwd_send_sem.at[k, i],
            fwd_recv_sem.at[k, s],
            (d + 1, cores[i]),
        )

    def to_before(i):
        return remote(
            send_back.at[i],
            recv_back.at[s],
            back_send_sem.at[i],
            back_recv_sem.at[s],
            (d - 1, cores[i]),
        )

    side = remote(send_side, mine.at[s], side_sem.at[0], side_sem.at[1], (d, 1 - s))

    placed1 = placed(sums)
    ahead = placed1 * scale(basis1[3])
    for i in range(2):
        send_fwd[1, i] = ahead[i * cap : (i + 1) * cap]

    pl.semaphore_wait(barrier, 1 + 2 * has_before.astype(jnp.int32) + 2 * has_after.astype(jnp.int32))

    @pl.when(jnp.logical_not(has_before))
    def _():
        recv_fwd[...] = jnp.zeros(recv_fwd.shape, F32)

    @pl.when(has_after)
    def _():
        for i in range(2):
            to_after(1, i).start()

    @pl.when(jnp.logical_not(has_after))
    def _():
        recv_back[...] = jnp.zeros(recv_back.shape, F32)

    sums = step_sums(0)
    placed0 = placed(sums)
    ahead = placed0 * scale(basis0[3]) + placed1 * scale(basis1[2])
    behind = placed0 * scale(basis0[0])
    for i in range(2):
        send_fwd[0, i] = ahead[i * cap : (i + 1) * cap]
        send_back[i] = behind[i * cap : (i + 1) * cap]

    @pl.when(has_after)
    def _():
        for i in range(2):
            to_after(0, i).start()

    @pl.when(has_before)
    def _():
        for i in range(2):
            to_before(i).start()

    for k in range(2):
        own = placed0 * scale(basis0[1 + k]) + placed1 * scale(basis1[k])
        mine[s, k] = own[:cap]
        send_side[k] = own[cap:]
    side.start()

    for copy in small[3:]:
        copy.wait()
    side.wait_send()
    remote(send_side, mine.at[1 - s], side_sem.at[0], side_sem.at[1], (d, 1 - s)).wait_recv()

    @pl.when(has_after)
    def _():
        for i in range(2):
            to_after(1, i).wait_send()
            to_after(0, i).wait_send()
            remote(
                send_back.at[i],
                recv_back.at[i],
                back_send_sem.at[i],
                back_recv_sem.at[i],
                (d + 1, i),
            ).wait_recv()

    @pl.when(has_before)
    def _():
        for i in range(2):
            to_before(i).wait_send()
            for k in range(2):
                remote(
                    send_fwd.at[k, i],
                    recv_fwd.at[k, i],
                    fwd_send_sem.at[k, i],
                    fwd_recv_sem.at[k, i],
                    (d - 1, i),
                ).wait_recv()

    for k in range(2):
        total = [mine[i, k] + recv_fwd[k, i] for i in range(2)]
        if k == 1:
            total = [total[i] + recv_back[i] for i in range(2)]
        parts = split3(jnp.concatenate(total, axis=0))
        table_h = spread[...]
        hess_ref[k] = sum(jnp.dot(part, table_h, preferred_element_type=F32) for part in parts)
        grad_ref[k] = sum(dot_nt(pick[...], part) for part in parts)


def per_device(n, n_space, image_gradient, residual, phase, counts, owner):
    steps, bricks, comps, voxels = image_gradient.shape
    cap = 3 * bricks // (2 * n_space)
    slots = n_space * cap
    hessian_lanes, gradient_lanes = spread_tables()
    hbm = pl.BlockSpec(memory_space=pltpu.HBM)
    vmem = pl.BlockSpec(memory_space=pltpu.VMEM)
    chunks = voxels // CHUNK
    dma = pltpu.SemaphoreType.DMA
    hess, grad = pl.pallas_call(
        functools.partial(kernel, n),
        out_shape=(
            jax.ShapeDtypeStruct((steps, slots, PATCH), F32),
            jax.ShapeDtypeStruct((steps, DOFS, slots), F32),
        ),
        in_specs=[hbm] * 8,
        out_specs=(vmem, vmem),
        scratch_shapes=[
            pltpu.VMEM((steps, comps, bricks, voxels), BF16),
            pltpu.VMEM((steps, bricks, voxels), BF16),
            pltpu.SMEM((steps,), F32),
            pltpu.VMEM((1, bricks), jnp.int32),
            pltpu.VMEM((1, bricks), jnp.int32),
            pltpu.VMEM((ROWS, voxels), BF16),
            pltpu.VMEM((LANES, PATCH), BF16),
            pltpu.VMEM((DOFS, LANES), BF16),
            pltpu.VMEM((bricks, voxels), BF16),
            pltpu.VMEM((ROWS, 9 * bricks), F32),
            pltpu.VMEM((2, 2, cap, LANES), F32),
            pltpu.VMEM((2, cap, LANES), F32),
            pltpu.VMEM((2, cap, LANES), F32),
            pltpu.VMEM((2, 2, cap, LANES), F32),
            pltpu.VMEM((2, cap, LANES), F32),
            pltpu.VMEM((2, 2, cap, LANES), F32),
            dma((3, 2, chunks)),
            dma((5,)),
            dma((2, 2)),
            dma((2, 2)),
            dma((2,)),
            dma((2,)),
            dma((2,)),
        ],
        compiler_params=pltpu.CompilerParams(
            collective_id=0, has_side_effects=True, vmem_limit_bytes=67043328
        ),
    )(
        jnp.transpose(image_gradient, (0, 2, 1, 3)),
        residual,
        phase,
        counts.reshape(1, bricks),
        owner.reshape(1, bricks),
        moment_table(),
        hessian_lanes,
        gradient_lanes,
    )
    return hess, jnp.transpose(grad, (0, 2, 1))


def solution(mesh):
    in_specs = (
        P("tm", "space", None, None),
        P("tm", "space", None),
        P("tm"),
        P("space"),
        P("space", None),
    )
    out_specs = (P("tm", "space", None), P("tm", "space", None))
    return jax.shard_map(
        functools.partial(per_device, mesh.shape["tm"], mesh.shape["space"]),
        mesh=mesh,
        in_specs=in_specs,
        out_specs=out_specs,
        check_vma=False,
    )
```

```python
import functools

import jax
import jax.numpy as jnp
import numpy as np
from jax import lax
from jax.experimental import pallas as pl
from jax.experimental.pallas import tpu as pltpu
from jax.sharding import PartitionSpec as P

EDGE = 16
COMPS = 3
NODES = 8
DOFS = NODES * COMPS
PATCH = DOFS * DOFS
MOMENTS = 27
PAIRS = ((0, 0), (0, 1), (0, 2), (1, 1), (1, 2), (2, 2))
ROWS = 80
LANES = 256
GRAD_LANE = 32 * len(PAIRS)
CHUNK = 1024
MESH = pl.DeviceIdType.MESH
F32 = jnp.float32
BF16 = jnp.bfloat16


def two_terms(table):
    high = table.astype(BF16)
    return high, (table - high.astype(np.float64)).astype(BF16)


def moment_table():
    voxel = np.arange(EDGE**3)
    axes = [voxel // (EDGE * EDGE), voxel // EDGE % EDGE, voxel % EDGE]
    u = [(axis + 0.5) / EDGE for axis in axes]
    quads = [((1 - x) ** 2, x * (1 - x), x * x) for x in u]
    lines = [(1 - x, x) for x in u]
    moments = np.stack([quads[0][m // 9] * quads[1][m // 3 % 3] * quads[2][m % 3] for m in range(MOMENTS)])
    shapes = np.stack([lines[0][a >> 2 & 1] * lines[1][a >> 1 & 1] * lines[2][a & 1] for a in range(NODES)])
    table = np.zeros((ROWS, EDGE**3), BF16)
    table[0:MOMENTS], table[32 : 32 + MOMENTS] = two_terms(moments)
    table[64:72], table[72:80] = two_terms(shapes)
    return table


def spread_tables():
    hessian = np.zeros((LANES, PATCH), np.float32)
    gradient = np.zeros((DOFS, LANES), np.float32)
    for a in range(NODES):
        for c in range(COMPS):
            gradient[COMPS * a + c, GRAD_LANE + NODES * c + a] = 1.0
            for b in range(NODES):
                for e in range(COMPS):
                    pair = PAIRS.index((min(c, e), max(c, e)))
                    bits = [(a >> s & 1) + (b >> s & 1) for s in (2, 1, 0)]
                    moment = bits[0] * 9 + bits[1] * 3 + bits[2]
                    hessian[32 * pair + moment, (COMPS * a + c) * DOFS + COMPS * b + e] = 1.0
    return hessian.astype(BF16), gradient.astype(BF16)


def split3(x):
    first = x.astype(BF16)
    rest = x - first.astype(F32)
    second = rest.astype(BF16)
    return first, second, (rest - second.astype(F32)).astype(BF16)


def dot_nt(a, b):
    return lax.dot_general(a, b, (((1,), (1,)), ((), ())), preferred_element_type=F32)


def kernel(
    n,
    image_hbm,
    resid_hbm,
    phase_hbm,
    counts_hbm,
    owner_hbm,
    table_hbm,
    spread_hbm,
    pick_hbm,
    total_ref,
    spread,
    pick,
    image,
    resid,
    phase,
    counts,
    owner,
    table,
    mask,
    acc,
    send_fwd,
    send_back,
    send_side,
    recv_fwd,
    recv_back,
    mine,
    load_sem,
    small_sem,
    fwd_send_sem,
    fwd_recv_sem,
    back_send_sem,
    back_recv_sem,
    side_sem,
):
    bricks, voxels = resid.shape[1], resid.shape[2]
    cap = mine.shape[2]
    chunks = voxels // CHUNK
    d = lax.axis_index("tm")
    s = lax.axis_index("space")
    has_before = d > 0
    has_after = d < n - 1

    small = [
        pltpu.make_async_copy(counts_hbm, counts, small_sem.at[0]),
        pltpu.make_async_copy(owner_hbm, owner, small_sem.at[1]),
        pltpu.make_async_copy(phase_hbm, phase, small_sem.at[2]),
        pltpu.make_async_copy(spread_hbm, spread, small_sem.at[3]),
        pltpu.make_async_copy(pick_hbm, pick, small_sem.at[4]),
    ]
    small[0].start()
    loads = {}
    for t in (1, 0):
        for k in range(chunks):
            span = pl.ds(k * CHUNK, CHUNK)
            loads[t, k] = [
                pltpu.make_async_copy(
                    image_hbm.at[t, :, :, span], image.at[t, :, :, span], load_sem.at[0, t, k]
                ),
                pltpu.make_async_copy(
                    resid_hbm.at[t, :, span], resid.at[t, :, span], load_sem.at[1, t, k]
                ),
            ]
            if t == 1:
                loads[t, k].append(
                    pltpu.make_async_copy(
                        table_hbm.at[:, span], table.at[:, span], load_sem.at[2, t, k]
                    )
                )
            for copy in loads[t, k]:
                copy.start()
    for copy in small[1:]:
        copy.start()

    barrier = pltpu.get_barrier_semaphore()

    def greet(where):
        pl.semaphore_signal(barrier, inc=1, device_id=where, device_id_type=MESH)

    greet((d, 1 - s))

    @pl.when(has_before)
    def _():
        greet((d - 1, 0))
        greet((d - 1, 1))

    @pl.when(has_after)
    def _():
        greet((d + 1, 0))
        greet((d + 1, 1))

    small[0].wait()
    square = lax.broadcasted_iota(jnp.int32, (bricks, bricks), 0) == lax.broadcasted_iota(
        jnp.int32, (bricks, bricks), 1
    )
    count_column = jnp.sum(
        jnp.where(square, jnp.broadcast_to(counts[...].astype(F32), (bricks, bricks)), 0.0),
        axis=1,
        keepdims=True,
    )
    for k in range(voxels // 512):
        voxel = (lax.broadcasted_iota(jnp.int32, (bricks, 512), 1) + k * 512).astype(F32)
        mask[:, k * 512 : (k + 1) * 512] = jnp.where(voxel < count_column, 1.0, 0.0).astype(BF16)

    def step_sums(t):
        for k in range(chunks):
            span = slice(k * CHUNK, (k + 1) * CHUNK)
            for copy in loads[t, k]:
                copy.wait()
            valid = mask[:, span]
            g = [image[t, c, :, span] * valid for c in range(COMPS)]
            r = resid[t, :, span]
            products = [g[c] * g[e] for c, e in PAIRS] + [g[c] * r for c in range(COMPS)]
            part = dot_nt(table[:, span], jnp.concatenate(products, axis=0))
            if k == 0:
                acc[...] = part
            else:
                acc[...] += part
        pairs = len(PAIRS) * bricks
        hess = acc[0:32, :pairs] + acc[32:64, :pairs]
        grad = acc[64:72, pairs:] + acc[72:80, pairs:]
        grad = jnp.concatenate([grad, jnp.zeros((8, bricks), F32)], axis=1)
        rows = []
        for q in range(len(PAIRS)):
            two = hess[:, 128 * (q // 2) : 128 * (q // 2) + 128]
            rows.append(pltpu.roll(two, 64, 1) if q % 2 else two)
        for c in range(COMPS):
            two = grad[:, 128 * (c // 2) : 128 * (c // 2) + 128]
            rows.append(pltpu.roll(two, 64, 1) if c % 2 else two)
        rows.append(jnp.zeros((LANES - GRAD_LANE - 24, 128), F32))
        return jnp.concatenate(rows, axis=0)

    sums = step_sums(1)

    for copy in small[1:3]:
        copy.wait()
    who = jnp.broadcast_to(owner[...].astype(F32), (8, bricks))
    earlier = lax.broadcasted_iota(jnp.int32, (bricks, bricks), 0) < lax.broadcasted_iota(
        jnp.int32, (bricks, bricks), 1
    )
    ones_before = jnp.dot(
        who.astype(BF16), jnp.where(earlier, 1.0, 0.0).astype(BF16), preferred_element_type=F32
    )
    place = lax.broadcasted_iota(jnp.int32, (8, bricks), 1).astype(F32)
    rank = jnp.where(who > 0.5, ones_before, place - ones_before)
    mine_first = jnp.where(s == 0, who, 1.0 - who)
    target = (mine_first * cap + rank)[0:1, :]
    slot = lax.broadcasted_iota(jnp.int32, (2 * cap, bricks), 0).astype(F32)
    hit = jnp.where(slot == jnp.broadcast_to(target, (2 * cap, bricks)), 1.0, 0.0)
    hit = jnp.concatenate([hit, jnp.zeros((2 * cap, 128 - bricks), F32)], axis=1).astype(BF16)

    def placed(x):
        a, b, c = split3(x)
        return dot_nt(hit, a) + dot_nt(hit, b) + dot_nt(hit, c)

    first = jnp.where(has_before, 0.0, 1.0)
    last = jnp.where(has_after, 0.0, 1.0)

    def weights(t):
        u = phase[t]
        v = 1.0 - u
        return (
            v * v * v * (1.0 / 6.0),
            (3.0 * u * u * u - 6.0 * u * u + 4.0) * (1.0 / 6.0),
            (-3.0 * u * u * u + 3.0 * u * u + 3.0 * u + 1.0) * (1.0 / 6.0),
            u * u * u * (1.0 / 6.0),
        )

    w = weights(0)
    basis0 = (w[0] * (1.0 - first), w[1] + first * w[0], w[2] + last * w[3], w[3] * (1.0 - last))
    w = weights(1)
    basis1 = (w[0], w[1] + last * (w[2] + w[3]), w[2] * (1.0 - last), w[3] * (1.0 - last))
    is_hess = lax.broadcasted_iota(jnp.int32, (1, LANES), 1) < GRAD_LANE

    def scale(b):
        return jnp.where(is_hess, b * b, b)

    def remote(src, dst, send_sem, recv_sem, where):
        return pltpu.make_async_remote_copy(
            src_ref=src,
            dst_ref=dst,
            send_sem=send_sem,
            recv_sem=recv_sem,
            device_id=where,
            device_id_type=MESH,
        )

    cores = (s, 1 - s)

    def to_after(k, i):
        return remote(
            send_fwd.at[k, i],
            recv_fwd.at[k, s],
            fwd_send_sem.at[k, i],
            fwd_recv_sem.at[k, s],
            (d + 1, cores[i]),
        )

    def to_before(i):
        return remote(
            send_back.at[i],
            recv_back.at[s],
            back_send_sem.at[i],
            back_recv_sem.at[s],
            (d - 1, cores[i]),
        )

    side = remote(send_side, mine.at[s], side_sem.at[0], side_sem.at[1], (d, 1 - s))

    placed1 = placed(sums)
    ahead = placed1 * scale(basis1[3])
    for i in range(2):
        send_fwd[1, i] = ahead[i * cap : (i + 1) * cap]

    pl.semaphore_wait(barrier, 1 + 2 * has_before.astype(jnp.int32) + 2 * has_after.astype(jnp.int32))

    @pl.when(jnp.logical_not(has_before))
    def _():
        recv_fwd[...] = jnp.zeros(recv_fwd.shape, F32)

    @pl.when(has_after)
    def _():
        for i in range(2):
            to_after(1, i).start()

    @pl.when(jnp.logical_not(has_after))
    def _():
        recv_back[...] = jnp.zeros(recv_back.shape, F32)

    sums = step_sums(0)
    placed0 = placed(sums)
    ahead = placed0 * scale(basis0[3]) + placed1 * scale(basis1[2])
    behind = placed0 * scale(basis0[0])
    for i in range(2):
        send_fwd[0, i] = ahead[i * cap : (i + 1) * cap]
        send_back[i] = behind[i * cap : (i + 1) * cap]

    @pl.when(has_after)
    def _():
        for i in range(2):
            to_after(0, i).start()

    @pl.when(has_before)
    def _():
        for i in range(2):
            to_before(i).start()

    for k in range(2):
        own = placed0 * scale(basis0[1 + k]) + placed1 * scale(basis1[k])
        mine[s, k] = own[:cap]
        send_side[k] = own[cap:]
    side.start()

    for copy in small[3:]:
        copy.wait()
    side.wait_send()
    remote(send_side, mine.at[1 - s], side_sem.at[0], side_sem.at[1], (d, 1 - s)).wait_recv()

    @pl.when(has_after)
    def _():
        for i in range(2):
            to_after(1, i).wait_send()
            to_after(0, i).wait_send()
            remote(
                send_back.at[i],
                recv_back.at[i],
                back_send_sem.at[i],
                back_recv_sem.at[i],
                (d + 1, i),
            ).wait_recv()

    @pl.when(has_before)
    def _():
        for i in range(2):
            to_before(i).wait_send()
            for k in range(2):
                remote(
                    send_fwd.at[k, i],
                    recv_fwd.at[k, i],
                    fwd_send_sem.at[k, i],
                    fwd_recv_sem.at[k, i],
                    (d - 1, i),
                ).wait_recv()

    for i in range(2):
        rows = slice(i * cap, (i + 1) * cap)
        total_ref[0, rows] = mine[i, 0] + recv_fwd[0, i]
        total_ref[1, rows] = mine[i, 1] + recv_fwd[1, i] + recv_back[i]


def spread_kernel(total_ref, spread, pick, hess_hbm, grad_hbm, hess, grad, sem):
    slots = total_ref.shape[1]
    half = slots // 2
    copies = []

    def store(src, dst):
        copies.append(pltpu.make_async_copy(src, dst, sem.at[len(copies)]))
        copies[-1].start()

    for k in range(2):
        parts = split3(total_ref[k])
        for i in range(2):
            rows = slice(i * half, (i + 1) * half)
            hess[k, rows] = sum(
                jnp.dot(part[rows], spread[...], preferred_element_type=F32) for part in parts
            )
            store(hess.at[k, rows], hess_hbm.at[k, rows])
        grad[k] = sum(dot_nt(pick[...], part) for part in parts)
        store(grad.at[k], grad_hbm.at[k])
    for copy in copies:
        copy.wait()


def per_device(n, n_space, image_gradient, residual, phase, counts, owner):
    steps, bricks, comps, voxels = image_gradient.shape
    cap = 3 * bricks // (2 * n_space)
    slots = n_space * cap
    hessian_lanes, gradient_lanes = spread_tables()
    hbm = pl.BlockSpec(memory_space=pltpu.HBM)
    vmem = pl.BlockSpec(memory_space=pltpu.VMEM)
    chunks = voxels // CHUNK
    dma = pltpu.SemaphoreType.DMA
    totals, spread, pick = pl.pallas_call(
        functools.partial(kernel, n),
        out_shape=(
            jax.ShapeDtypeStruct((steps, slots, LANES), F32),
            jax.ShapeDtypeStruct((LANES, PATCH), BF16),
            jax.ShapeDtypeStruct((DOFS, LANES), BF16),
        ),
        in_specs=[hbm] * 8,
        out_specs=(vmem, vmem, vmem),
        scratch_shapes=[
            pltpu.VMEM((steps, comps, bricks, voxels), BF16),
            pltpu.VMEM((steps, bricks, voxels), BF16),
            pltpu.SMEM((steps,), F32),
            pltpu.VMEM((1, bricks), jnp.int32),
            pltpu.VMEM((1, bricks), jnp.int32),
            pltpu.VMEM((ROWS, voxels), BF16),
            pltpu.VMEM((bricks, voxels), BF16),
            pltpu.VMEM((ROWS, 9 * bricks), F32),
            pltpu.VMEM((2, 2, cap, LANES), F32),
            pltpu.VMEM((2, cap, LANES), F32),
            pltpu.VMEM((2, cap, LANES), F32),
            pltpu.VMEM((2, 2, cap, LANES), F32),
            pltpu.VMEM((2, cap, LANES), F32),
            pltpu.VMEM((2, 2, cap, LANES), F32),
            dma((3, 2, chunks)),
            dma((5,)),
            dma((2, 2)),
            dma((2, 2)),
            dma((2,)),
            dma((2,)),
            dma((2,)),
        ],
        compiler_params=pltpu.CompilerParams(
            collective_id=0, has_side_effects=True, vmem_limit_bytes=40 << 20
        ),
    )(
        *[
            pltpu.with_memory_space_constraint(x, pltpu.HBM)
            for x in (
                jnp.transpose(image_gradient, (0, 2, 1, 3)),
                residual,
                phase,
                counts.reshape(1, bricks),
                owner.reshape(1, bricks),
                jnp.asarray(moment_table()),
                jnp.asarray(hessian_lanes),
                jnp.asarray(gradient_lanes),
            )
        ]
    )
    hess, grad = pl.pallas_call(
        spread_kernel,
        out_shape=(
            jax.ShapeDtypeStruct((steps, slots, PATCH), F32),
            jax.ShapeDtypeStruct((steps, DOFS, slots), F32),
        ),
        in_specs=[vmem] * 3,
        out_specs=(hbm, hbm),
        scratch_shapes=[
            pltpu.VMEM((steps, slots, PATCH), F32),
            pltpu.VMEM((steps, DOFS, slots), F32),
            dma((3 * steps,)),
        ],
        compiler_params=pltpu.CompilerParams(vmem_limit_bytes=16 << 20),
    )(totals, spread, pick)
    return hess, jnp.transpose(grad, (0, 2, 1))


def solution(mesh):
    in_specs = (
        P("tm", "space", None, None),
        P("tm", "space", None),
        P("tm"),
        P("space"),
        P("space", None),
    )
    out_specs = (P("tm", "space", None), P("tm", "space", None))
    return jax.shard_map(
        functools.partial(per_device, mesh.shape["tm"], mesh.shape["space"]),
        mesh=mesh,
        in_specs=in_specs,
        out_specs=out_specs,
        check_vma=False,
    )
```

```python
import functools

import jax
import jax.numpy as jnp
import numpy as np
from jax import lax
from jax.experimental import pallas as pl
from jax.experimental.pallas import tpu as pltpu
from jax.sharding import PartitionSpec as P

EDGE = 16
COMPS = 3
NODES = 8
DOFS = NODES * COMPS
PATCH = DOFS * DOFS
MOMENTS = 27
PAIRS = ((0, 0), (0, 1), (0, 2), (1, 1), (1, 2), (2, 2))
TILE = 256
BLOCK = 32
CHUNK = 1024
MESH = pl.DeviceIdType.MESH
F32 = jnp.float32
BF16 = jnp.bfloat16


def two_terms(table):
    high = table.astype(BF16)
    return high, (table - high.astype(np.float64)).astype(BF16)


def moment_table():
    voxel = np.arange(EDGE**3)
    axes = [voxel // (EDGE * EDGE), voxel // EDGE % EDGE, voxel % EDGE]
    u = [(axis + 0.5) / EDGE for axis in axes]
    quads = [((1 - x) ** 2, x * (1 - x), x * x) for x in u]
    lines = [(1 - x, x) for x in u]
    exact = np.zeros((EDGE**3, 128))
    for block in range(4):
        for m in range(MOMENTS):
            exact[:, BLOCK * block + m] = quads[0][m // 9] * quads[1][m // 3 % 3] * quads[2][m % 3]
        for i in range(4):
            a = 4 * (block % 2) + i
            exact[:, BLOCK * block + MOMENTS + i] = (
                lines[0][a >> 2 & 1] * lines[1][a >> 1 & 1] * lines[2][a & 1]
            )
    return np.concatenate(two_terms(exact), axis=1)


def spread_tables():
    hessian = np.zeros((256, PATCH), np.float32)
    gradient = np.zeros((DOFS, 256), np.float32)
    for a in range(NODES):
        for c in range(COMPS):
            gradient[COMPS * a + c, BLOCK * (2 * c + a // 4) + MOMENTS + a % 4] = 1.0
            for b in range(NODES):
                for e in range(COMPS):
                    pair = PAIRS.index((min(c, e), max(c, e)))
                    bits = [(a >> s & 1) + (b >> s & 1) for s in (2, 1, 0)]
                    moment = bits[0] * 9 + bits[1] * 3 + bits[2]
                    hessian[BLOCK * pair + moment, (COMPS * a + c) * DOFS + COMPS * b + e] = 1.0
    hessian[192:] = hessian[128:192]
    gradient[:, 192:] = gradient[:, 128:192]
    return hessian.astype(BF16), gradient.astype(BF16)


def split3(x):
    first = x.astype(BF16)
    rest = x - first.astype(F32)
    second = rest.astype(BF16)
    return first, second, (rest - second.astype(F32)).astype(BF16)


def dot_nt(a, b):
    return lax.dot_general(a, b, (((1,), (1,)), ((), ())), preferred_element_type=F32)


def kernel(
    n,
    image_hbm,
    resid_hbm,
    phase_hbm,
    counts_hbm,
    owner_hbm,
    table_hbm,
    spread_hbm,
    pick_hbm,
    total_ref,
    spread,
    pick,
    image,
    resid,
    phase,
    counts,
    owner,
    table,
    mask,
    send_fwd,
    send_back,
    send_side,
    recv_fwd,
    recv_back,
    mine,
    load_sem,
    small_sem,
    fwd_send_sem,
    fwd_recv_sem,
    back_send_sem,
    back_recv_sem,
    side_sem,
):
    bricks, voxels = resid.shape[1], resid.shape[2]
    cap = 2 * mine.shape[2] // 3
    half = cap // 2
    chunks = voxels // CHUNK
    d = lax.axis_index("tm")
    s = lax.axis_index("space")
    has_before = d > 0
    has_after = d < n - 1

    small = [
        pltpu.make_async_copy(counts_hbm, counts, small_sem.at[0]),
        pltpu.make_async_copy(owner_hbm, owner, small_sem.at[1]),
        pltpu.make_async_copy(phase_hbm, phase, small_sem.at[2]),
        pltpu.make_async_copy(spread_hbm, spread, small_sem.at[3]),
        pltpu.make_async_copy(pick_hbm, pick, small_sem.at[4]),
    ]
    small[0].start()
    loads = {}
    for t in (1, 0):
        for k in range(chunks):
            span = pl.ds(k * CHUNK, CHUNK)
            loads[t, k] = [
                pltpu.make_async_copy(
                    image_hbm.at[t, :, :, span], image.at[t, :, :, span], load_sem.at[0, t, k]
                ),
                pltpu.make_async_copy(
                    resid_hbm.at[t, :, span], resid.at[t, :, span], load_sem.at[1, t, k]
                ),
            ]
            if t == 1:
                loads[t, k].append(
                    pltpu.make_async_copy(
                        table_hbm.at[span], table.at[span], load_sem.at[2, t, k]
                    )
                )
            for copy in loads[t, k]:
                copy.start()
    for copy in small[1:]:
        copy.start()

    barrier = pltpu.get_barrier_semaphore()

    def greet(where):
        pl.semaphore_signal(barrier, inc=1, device_id=where, device_id_type=MESH)

    greet((d, 1 - s))

    @pl.when(has_before)
    def _():
        greet((d - 1, 0))
        greet((d - 1, 1))

    @pl.when(has_after)
    def _():
        greet((d + 1, 0))
        greet((d + 1, 1))

    small[0].wait()
    square = lax.broadcasted_iota(jnp.int32, (bricks, bricks), 0) == lax.broadcasted_iota(
        jnp.int32, (bricks, bricks), 1
    )
    count_column = jnp.sum(
        jnp.where(square, jnp.broadcast_to(counts[...].astype(F32), (bricks, bricks)), 0.0),
        axis=1,
        keepdims=True,
    )
    for k in range(voxels // 512):
        voxel = (lax.broadcasted_iota(jnp.int32, (bricks, 512), 1) + k * 512).astype(F32)
        mask[:, k * 512 : (k + 1) * 512] = jnp.where(voxel < count_column, 1.0, 0.0).astype(BF16)

    lane = lax.broadcasted_iota(jnp.int32, (1, 128), 1)
    spare = lane % BLOCK >= MOMENTS

    def step_sums(t):
        def sums(*accs):
            for tile in range(voxels // TILE):
                if tile * TILE % CHUNK == 0:
                    for copy in loads[t, tile * TILE // CHUNK]:
                        copy.wait()
                unit, staging = tile % 2, tile // 2 % 2
                span = slice(tile * TILE, (tile + 1) * TILE)
                pltpu.matmul_push_rhs(table[span, :], staging, unit)
                valid = mask[:, span]
                g = [image[t, c, :, span] * valid for c in range(COMPS)]
                r = resid[t, :, span]
                products = [g[c] * g[e] for c, e in PAIRS] + [g[c] * r for c in range(COMPS)]
                for q, product in enumerate(products):
                    pltpu.matmul_acc_lhs(accs[9 * unit + q], product, staging if q == 0 else None)
            found = []
            for q in range(9):
                both = pltpu.matmul_pop(accs[q]) + pltpu.matmul_pop(accs[9 + q])
                found.append(both[:, :128] + both[:, 128:])
            return found

        found = pl.run_scoped(
            sums, *[pltpu.ACC(unit)((bricks, 256), F32) for unit in range(2) for _ in range(9)]
        )
        first = jnp.where(lane < 2 * BLOCK, found[6], found[7])
        for q in range(4):
            first = jnp.where(jnp.logical_and(lane // BLOCK == q, jnp.logical_not(spare)), found[q], first)
        second = jnp.where(spare, found[8], jnp.where(lane // BLOCK % 2 == 0, found[4], found[5]))
        return jnp.concatenate([first, second], axis=1)

    sums = step_sums(1)

    for copy in small[1:3]:
        copy.wait()
    who = owner[...].astype(F32)
    who_column = jnp.sum(
        jnp.where(square, jnp.broadcast_to(who, (bricks, bricks)), 0.0), axis=1, keepdims=True
    )
    earlier = lax.broadcasted_iota(jnp.int32, (bricks, bricks), 0) < lax.broadcasted_iota(
        jnp.int32, (bricks, bricks), 1
    )
    ones_before = jnp.sum(jnp.where(earlier, who_column, 0.0), axis=0, keepdims=True)
    place = lax.broadcasted_iota(jnp.int32, (1, bricks), 1).astype(F32)
    rank = jnp.where(who > 0.5, ones_before, place - ones_before)
    mine_first = jnp.where(s == 0, who, 1.0 - who)
    target = mine_first * cap + rank
    slot = lax.broadcasted_iota(jnp.int32, (2 * cap, bricks), 0).astype(F32)
    hit = jnp.where(slot == jnp.broadcast_to(target, (2 * cap, bricks)), 1.0, 0.0)
    hit = hit.astype(BF16)
    hits = jnp.concatenate([hit, hit, hit, jnp.zeros_like(hit)], axis=1)

    def placed(x):
        def product(acc):
            pltpu.matmul_push_rhs(
                jnp.concatenate([*split3(x), jnp.zeros(x.shape, BF16)], axis=0), 0, 0
            )
            pltpu.matmul_acc_lhs(acc, hits, 0)
            return pltpu.matmul_pop(acc)

        rows = pl.run_scoped(product, pltpu.ACC(0)((2 * cap, 256), F32))
        out = []
        for i in range(2):
            part = rows[i * cap : (i + 1) * cap]
            out.append(part[:, :128])
            out.append(jnp.where(lane < 64, part[:half, 128:], part[half:, 128:]))
        return jnp.concatenate(out, axis=0)

    first = jnp.where(has_before, 0.0, 1.0)
    last = jnp.where(has_after, 0.0, 1.0)

    def weights(t):
        u = phase[t]
        v = 1.0 - u
        return (
            v * v * v * (1.0 / 6.0),
            (3.0 * u * u * u - 6.0 * u * u + 4.0) * (1.0 / 6.0),
            (-3.0 * u * u * u + 3.0 * u * u + 3.0 * u + 1.0) * (1.0 / 6.0),
            u * u * u * (1.0 / 6.0),
        )

    w = weights(0)
    basis0 = (w[0] * (1.0 - first), w[1] + first * w[0], w[2] + last * w[3], w[3] * (1.0 - last))
    w = weights(1)
    basis1 = (w[0], w[1] + last * (w[2] + w[3]), w[2] * (1.0 - last), w[3] * (1.0 - last))
    size = cap + half

    def scale(b):
        return jnp.where(spare, b, b * b)

    def remote(src, dst, send_sem, recv_sem, where):
        return pltpu.make_async_remote_copy(
            src_ref=src,
            dst_ref=dst,
            send_sem=send_sem,
            recv_sem=recv_sem,
            device_id=where,
            device_id_type=MESH,
        )

    cores = (s, 1 - s)

    def to_after(k, i):
        return remote(
            send_fwd.at[k, i],
            recv_fwd.at[k, s],
            fwd_send_sem.at[k, i],
            fwd_recv_sem.at[k, s],
            (d + 1, cores[i]),
        )

    def to_before(i):
        return remote(
            send_back.at[i],
            recv_back.at[s],
            back_send_sem.at[i],
            back_recv_sem.at[s],
            (d - 1, cores[i]),
        )

    side = remote(send_side, mine.at[s], side_sem.at[0], side_sem.at[1], (d, 1 - s))

    placed1 = placed(sums)
    ahead = placed1 * scale(basis1[3])
    for i in range(2):
        send_fwd[1, i] = ahead[i * size : (i + 1) * size]

    pl.semaphore_wait(barrier, 1 + 2 * has_before.astype(jnp.int32) + 2 * has_after.astype(jnp.int32))

    @pl.when(jnp.logical_not(has_before))
    def _():
        recv_fwd[...] = jnp.zeros(recv_fwd.shape, F32)

    @pl.when(has_after)
    def _():
        for i in range(2):
            to_after(1, i).start()

    @pl.when(jnp.logical_not(has_after))
    def _():
        recv_back[...] = jnp.zeros(recv_back.shape, F32)

    sums = step_sums(0)
    placed0 = placed(sums)
    ahead = placed0 * scale(basis0[3]) + placed1 * scale(basis1[2])
    behind = placed0 * scale(basis0[0])
    for i in range(2):
        send_fwd[0, i] = ahead[i * size : (i + 1) * size]
        send_back[i] = behind[i * size : (i + 1) * size]

    @pl.when(has_after)
    def _():
        for i in range(2):
            to_after(0, i).start()

    @pl.when(has_before)
    def _():
        for i in range(2):
            to_before(i).start()

    for k in range(2):
        own = placed0 * scale(basis0[1 + k]) + placed1 * scale(basis1[k])
        mine[s, k] = own[:size]
        send_side[k] = own[size:]
    side.start()

    for copy in small[3:]:
        copy.wait()
    remote(send_side, mine.at[1 - s], side_sem.at[0], side_sem.at[1], (d, 1 - s)).wait_recv()

    @pl.when(has_after)
    def _():
        for i in range(2):
            remote(
                send_back.at[i],
                recv_back.at[i],
                back_send_sem.at[i],
                back_recv_sem.at[i],
                (d + 1, i),
            ).wait_recv()

    @pl.when(has_before)
    def _():
        for i in range(2):
            for k in range(2):
                remote(
                    send_fwd.at[k, i],
                    recv_fwd.at[k, i],
                    fwd_send_sem.at[k, i],
                    fwd_recv_sem.at[k, i],
                    (d - 1, i),
                ).wait_recv()

    for i in range(2):
        total_ref[0, i] = mine[i, 0] + recv_fwd[0, i]
        total_ref[1, i] = mine[i, 1] + recv_fwd[1, i] + recv_back[i]

    side.wait_send()

    @pl.when(has_after)
    def _():
        for i in range(2):
            to_after(1, i).wait_send()
            to_after(0, i).wait_send()

    @pl.when(has_before)
    def _():
        for i in range(2):
            to_before(i).wait_send()


def spread_kernel(total_ref, spread, pick, hess_hbm, grad_hbm, hess, grad, sem):
    cap = 2 * total_ref.shape[2] // 3
    half = cap // 2
    lane = lax.broadcasted_iota(jnp.int32, (1, 128), 1)
    copies = []

    def store(src, dst):
        copies.append(pltpu.make_async_copy(src, dst, sem.at[len(copies)]))
        copies[-1].start()

    for k in range(2):
        wide = []
        for i in range(2):
            tail = total_ref[k, i, cap:]
            for j in range(2):
                kept = jnp.where((lane < 64) == (j == 0), tail, 0.0)
                wide.append(
                    jnp.concatenate([total_ref[k, i, j * half : (j + 1) * half], kept], axis=1)
                )
        parts = split3(jnp.concatenate(wide, axis=0))
        for i in range(2):
            rows = slice(i * cap, (i + 1) * cap)
            hess[k, rows] = sum(
                jnp.dot(part[rows], spread[...], preferred_element_type=F32) for part in parts
            )
            store(hess.at[k, rows], hess_hbm.at[k, rows])
        grad[k] = sum(dot_nt(pick[...], part) for part in parts)
        store(grad.at[k], grad_hbm.at[k])
    for copy in copies:
        copy.wait()


def per_device(n, n_space, image_gradient, residual, phase, counts, owner):
    steps, bricks, comps, voxels = image_gradient.shape
    cap = 3 * bricks // (2 * n_space)
    slots = n_space * cap
    size = cap + cap // 2
    hessian_lanes, gradient_lanes = spread_tables()
    hbm = pl.BlockSpec(memory_space=pltpu.HBM)
    vmem = pl.BlockSpec(memory_space=pltpu.VMEM)
    chunks = voxels // CHUNK
    dma = pltpu.SemaphoreType.DMA
    totals, spread, pick = pl.pallas_call(
        functools.partial(kernel, n),
        out_shape=(
            jax.ShapeDtypeStruct((steps, 2, size, 128), F32),
            jax.ShapeDtypeStruct((256, PATCH), BF16),
            jax.ShapeDtypeStruct((DOFS, 256), BF16),
        ),
        in_specs=[hbm] * 8,
        out_specs=(vmem, vmem, vmem),
        scratch_shapes=[
            pltpu.VMEM((steps, comps, bricks, voxels), BF16),
            pltpu.VMEM((steps, bricks, voxels), BF16),
            pltpu.SMEM((steps,), F32),
            pltpu.VMEM((1, bricks), jnp.int32),
            pltpu.VMEM((1, bricks), jnp.int32),
            pltpu.VMEM((voxels, 256), BF16),
            pltpu.VMEM((bricks, voxels), BF16),
            pltpu.VMEM((2, 2, size, 128), F32),
            pltpu.VMEM((2, size, 128), F32),
            pltpu.VMEM((2, size, 128), F32),
            pltpu.VMEM((2, 2, size, 128), F32),
            pltpu.VMEM((2, size, 128), F32),
            pltpu.VMEM((2, 2, size, 128), F32),
            dma((3, 2, chunks)),
            dma((5,)),
            dma((2, 2)),
            dma((2, 2)),
            dma((2,)),
            dma((2,)),
            dma((2,)),
        ],
        compiler_params=pltpu.CompilerParams(
            collective_id=0, has_side_effects=True, vmem_limit_bytes=40 << 20
        ),
    )(
        *[
            pltpu.with_memory_space_constraint(x, pltpu.HBM)
            for x in (
                jnp.transpose(image_gradient, (0, 2, 1, 3)),
                residual,
                phase,
                counts.reshape(1, bricks),
                owner.reshape(1, bricks),
                jnp.asarray(moment_table()),
                jnp.asarray(hessian_lanes),
                jnp.asarray(gradient_lanes),
            )
        ]
    )
    hess, grad = pl.pallas_call(
        spread_kernel,
        out_shape=(
            jax.ShapeDtypeStruct((steps, slots, PATCH), F32),
            jax.ShapeDtypeStruct((steps, DOFS, slots), F32),
        ),
        in_specs=[vmem] * 3,
        out_specs=(hbm, hbm),
        scratch_shapes=[
            pltpu.VMEM((steps, slots, PATCH), F32),
            pltpu.VMEM((steps, DOFS, slots), F32),
            dma((3 * steps,)),
        ],
        compiler_params=pltpu.CompilerParams(vmem_limit_bytes=16 << 20),
    )(totals, spread, pick)
    return hess, jnp.transpose(grad, (0, 2, 1))


def solution(mesh):
    in_specs = (
        P("tm", "space", None, None),
        P("tm", "space", None),
        P("tm"),
        P("space"),
        P("space", None),
    )
    out_specs = (P("tm", "space", None), P("tm", "space", None))
    return jax.shard_map(
        functools.partial(per_device, mesh.shape["tm"], mesh.shape["space"]),
        mesh=mesh,
        in_specs=in_specs,
        out_specs=out_specs,
        check_vma=False,
    )
```

```python
import functools

import jax
import jax.numpy as jnp
import numpy as np
from jax import lax
from jax.experimental import pallas as pl
from jax.experimental.pallas import tpu as pltpu
from jax.sharding import PartitionSpec as P

EDGE = 16
COMPS = 3
NODES = 8
DOFS = NODES * COMPS
PATCH = DOFS * DOFS
MOMENTS = 27
PAIRS = ((0, 0), (0, 1), (0, 2), (1, 1), (1, 2), (2, 2))
TILE = 256
BLOCK = 32
CHUNKS = ((2048, 2048), (1024, 1024, 2048))
AHEAD = 6
MESH = pl.DeviceIdType.MESH
F32 = jnp.float32
BF16 = jnp.bfloat16


def two_terms(table):
    high = table.astype(BF16)
    return high, (table - high.astype(np.float64)).astype(BF16)


def moment_table():
    voxel = np.arange(EDGE**3)
    axes = [voxel // (EDGE * EDGE), voxel // EDGE % EDGE, voxel % EDGE]
    u = [(axis + 0.5) / EDGE for axis in axes]
    quads = [((1 - x) ** 2, x * (1 - x), x * x) for x in u]
    lines = [(1 - x, x) for x in u]
    exact = np.zeros((EDGE**3, 128))
    for block in range(4):
        for m in range(MOMENTS):
            exact[:, BLOCK * block + m] = quads[0][m // 9] * quads[1][m // 3 % 3] * quads[2][m % 3]
        for i in range(4):
            a = 4 * (block % 2) + i
            exact[:, BLOCK * block + MOMENTS + i] = (
                lines[0][a >> 2 & 1] * lines[1][a >> 1 & 1] * lines[2][a & 1]
            )
    return np.concatenate(two_terms(exact), axis=1)


def spread_tables():
    hessian = np.zeros((256, PATCH), np.float32)
    gradient = np.zeros((DOFS, 256), np.float32)
    for a in range(NODES):
        for c in range(COMPS):
            gradient[COMPS * a + c, BLOCK * (2 * c + a // 4) + MOMENTS + a % 4] = 1.0
            for b in range(NODES):
                for e in range(COMPS):
                    pair = PAIRS.index((min(c, e), max(c, e)))
                    bits = [(a >> s & 1) + (b >> s & 1) for s in (2, 1, 0)]
                    moment = bits[0] * 9 + bits[1] * 3 + bits[2]
                    hessian[BLOCK * pair + moment, (COMPS * a + c) * DOFS + COMPS * b + e] = 1.0
    hessian[192:] = hessian[128:192]
    gradient[:, 192:] = gradient[:, 128:192]
    return hessian.astype(BF16), gradient.astype(BF16)


def split3(x):
    first = x.astype(BF16)
    rest = x - first.astype(F32)
    second = rest.astype(BF16)
    return first, second, (rest - second.astype(F32)).astype(BF16)


def split2(x):
    first = x.astype(BF16)
    return first, (x - first.astype(F32)).astype(BF16)


def dot_nt(a, b):
    return lax.dot_general(a, b, (((1,), (1,)), ((), ())), preferred_element_type=F32)


def kernel(
    n,
    image_hbm,
    resid_hbm,
    phase_hbm,
    counts_hbm,
    owner_hbm,
    table_hbm,
    spread_hbm,
    pick_hbm,
    total_ref,
    spread,
    pick,
    image,
    resid,
    phase,
    counts,
    owner,
    table,
    mask,
    send_fwd,
    send_back,
    send_side,
    recv_fwd,
    recv_back,
    mine,
    load_sem,
    small_sem,
    fwd_send_sem,
    fwd_recv_sem,
    back_send_sem,
    back_recv_sem,
    side_sem,
):
    bricks, voxels = resid.shape[1], resid.shape[2]
    cap = 2 * mine.shape[2] // 3
    half = cap // 2
    d = lax.axis_index("tm")
    s = lax.axis_index("space")
    has_before = d > 0
    has_after = d < n - 1

    small = [
        pltpu.make_async_copy(counts_hbm, counts, small_sem.at[0]),
        pltpu.make_async_copy(owner_hbm, owner, small_sem.at[1]),
        pltpu.make_async_copy(phase_hbm, phase, small_sem.at[2]),
        pltpu.make_async_copy(spread_hbm, spread, small_sem.at[3]),
        pltpu.make_async_copy(pick_hbm, pick, small_sem.at[4]),
    ]
    small[0].start()
    loads = {}
    for t in (1, 0):
        for k, size in enumerate(CHUNKS[t]):
            span = pl.ds(sum(CHUNKS[t][:k]), size)
            loads[t, k] = [
                pltpu.make_async_copy(
                    image_hbm.at[t, :, :, span], image.at[t, :, :, span], load_sem.at[0, t, k]
                ),
                pltpu.make_async_copy(
                    resid_hbm.at[t, :, span], resid.at[t, :, span], load_sem.at[1, t, k]
                ),
            ]
            if t == 1:
                loads[t, k].append(
                    pltpu.make_async_copy(
                        table_hbm.at[span], table.at[span], load_sem.at[2, t, k]
                    )
                )
            for copy in loads[t, k]:
                copy.start()
    for copy in small[1:]:
        copy.start()

    barrier = pltpu.get_barrier_semaphore()

    def greet(where):
        pl.semaphore_signal(barrier, inc=1, device_id=where, device_id_type=MESH)

    greet((d, 1 - s))

    @pl.when(has_before)
    def _():
        greet((d - 1, 0))
        greet((d - 1, 1))

    @pl.when(has_after)
    def _():
        greet((d + 1, 0))
        greet((d + 1, 1))

    small[0].wait()
    square = lax.broadcasted_iota(jnp.int32, (bricks, bricks), 0) == lax.broadcasted_iota(
        jnp.int32, (bricks, bricks), 1
    )
    count_column = jnp.sum(
        jnp.where(square, jnp.broadcast_to(counts[...].astype(F32), (bricks, bricks)), 0.0),
        axis=1,
        keepdims=True,
    )
    for k in range(voxels // 512):
        voxel = (lax.broadcasted_iota(jnp.int32, (bricks, 512), 1) + k * 512).astype(F32)
        mask[:, k * 512 : (k + 1) * 512] = jnp.where(voxel < count_column, 1.0, 0.0).astype(BF16)

    lane = lax.broadcasted_iota(jnp.int32, (1, 128), 1)
    spare = lane % BLOCK >= MOMENTS

    def add_tiles(t, accs, begin, end):
        for tile in range(begin, end):
            unit, staging = tile % 2, tile // 2 % 2
            span = slice(tile * TILE, (tile + 1) * TILE)
            pltpu.matmul_push_rhs(table[span, :], staging, unit)
            valid = mask[:, span]
            g = [image[t, c, :, span] * valid for c in range(COMPS)]
            r = resid[t, :, span]
            products = [g[c] * g[e] for c, e in PAIRS] + [g[c] * r for c in range(COMPS)]
            for q, product in enumerate(products):
                pltpu.matmul_acc_lhs(accs[9 * unit + q], product, staging if q == 0 else None)

    def pop_sums(accs):
        found = []
        for q in range(9):
            both = pltpu.matmul_pop(accs[q]) + pltpu.matmul_pop(accs[9 + q])
            found.append(both[:, :128] + both[:, 128:])
        return found

    def arranged(found):
        first = jnp.where(lane < 2 * BLOCK, found[6], found[7])
        for q in range(4):
            first = jnp.where(jnp.logical_and(lane // BLOCK == q, jnp.logical_not(spare)), found[q], first)
        second = jnp.where(spare, found[8], jnp.where(lane // BLOCK % 2 == 0, found[4], found[5]))
        return jnp.concatenate([first, second], axis=1)


    for copy in small[1:3]:
        copy.wait()
    who = owner[...].astype(F32)
    who_column = jnp.sum(
        jnp.where(square, jnp.broadcast_to(who, (bricks, bricks)), 0.0), axis=1, keepdims=True
    )
    earlier = lax.broadcasted_iota(jnp.int32, (bricks, bricks), 0) < lax.broadcasted_iota(
        jnp.int32, (bricks, bricks), 1
    )
    ones_before = jnp.sum(jnp.where(earlier, who_column, 0.0), axis=0, keepdims=True)
    place = lax.broadcasted_iota(jnp.int32, (1, bricks), 1).astype(F32)
    rank = jnp.where(who > 0.5, ones_before, place - ones_before)
    mine_first = jnp.where(s == 0, who, 1.0 - who)
    target = mine_first * cap + rank
    slot = lax.broadcasted_iota(jnp.int32, (2 * cap, bricks), 0).astype(F32)
    hit = jnp.where(slot == jnp.broadcast_to(target, (2 * cap, bricks)), 1.0, 0.0)
    hit = hit.astype(BF16)
    hits = jnp.concatenate([hit, hit, hit, jnp.zeros_like(hit)], axis=1)

    def placed(x, acc):
        pltpu.matmul_push_rhs(
            jnp.concatenate([*split3(x), jnp.zeros(x.shape, BF16)], axis=0), 0, 0
        )
        pltpu.matmul_acc_lhs(acc, hits, 0)
        rows = pltpu.matmul_pop(acc)
        out = []
        for i in range(2):
            part = rows[i * cap : (i + 1) * cap]
            out.append(part[:, :128])
            out.append(jnp.where(lane < 64, part[:half, 128:], part[half:, 128:]))
        return jnp.concatenate(out, axis=0)

    first = jnp.where(has_before, 0.0, 1.0)
    last = jnp.where(has_after, 0.0, 1.0)

    def weights(t):
        u = phase[t]
        v = 1.0 - u
        return (
            v * v * v * (1.0 / 6.0),
            (3.0 * u * u * u - 6.0 * u * u + 4.0) * (1.0 / 6.0),
            (-3.0 * u * u * u + 3.0 * u * u + 3.0 * u + 1.0) * (1.0 / 6.0),
            u * u * u * (1.0 / 6.0),
        )

    w = weights(0)
    basis0 = (w[0] * (1.0 - first), w[1] + first * w[0], w[2] + last * w[3], w[3] * (1.0 - last))
    w = weights(1)
    basis1 = (w[0], w[1] + last * (w[2] + w[3]), w[2] * (1.0 - last), w[3] * (1.0 - last))
    size = cap + half

    def scale(b):
        return jnp.where(spare, b, b * b)

    def remote(src, dst, send_sem, recv_sem, where):
        return pltpu.make_async_remote_copy(
            src_ref=src,
            dst_ref=dst,
            send_sem=send_sem,
            recv_sem=recv_sem,
            device_id=where,
            device_id_type=MESH,
        )

    cores = (s, 1 - s)

    def to_after(k, i):
        return remote(
            send_fwd.at[k, i],
            recv_fwd.at[k, s],
            fwd_send_sem.at[k, i],
            fwd_recv_sem.at[k, s],
            (d + 1, cores[i]),
        )

    def to_before(i):
        return remote(
            send_back.at[i],
            recv_back.at[s],
            back_send_sem.at[i],
            back_recv_sem.at[s],
            (d - 1, cores[i]),
        )

    side = remote(send_side, mine.at[s], side_sem.at[0], side_sem.at[1], (d, 1 - s))

    def send_second(placed1):
        ahead = placed1 * scale(basis1[3])
        for i in range(2):
            send_fwd[1, i] = ahead[i * size : (i + 1) * size]

        pl.semaphore_wait(barrier, 1 + 2 * has_before.astype(jnp.int32) + 2 * has_after.astype(jnp.int32))

        @pl.when(jnp.logical_not(has_before))
        def _():
            recv_fwd[...] = jnp.zeros(recv_fwd.shape, F32)

        @pl.when(has_after)
        def _():
            for i in range(2):
                to_after(1, i).start()

        @pl.when(jnp.logical_not(has_after))
        def _():
            recv_back[...] = jnp.zeros(recv_back.shape, F32)

    tiles = voxels // TILE

    def second_step(*accs):
        done = 0
        for k, voxel_count in enumerate(CHUNKS[1]):
            for copy in loads[1, k]:
                copy.wait()
            add_tiles(1, accs, done, done + voxel_count // TILE)
            done += voxel_count // TILE
        return pop_sums(accs)

    def first_step(place_acc, *accs):
        for k in range(len(CHUNKS[0])):
            for copy in loads[0, k]:
                copy.wait()
        add_tiles(0, accs, 0, AHEAD)
        placed1 = placed(arranged(found), place_acc)
        send_second(placed1)
        add_tiles(0, accs, AHEAD, tiles)
        return placed1, placed(arranged(pop_sums(accs)), place_acc)

    sums_acc = [pltpu.ACC(unit)((bricks, 256), F32) for unit in range(2) for _ in range(9)]
    found = pl.run_scoped(second_step, *sums_acc)
    placed1, placed0 = pl.run_scoped(first_step, pltpu.ACC(0)((2 * cap, 256), F32), *sums_acc)
    ahead = placed0 * scale(basis0[3]) + placed1 * scale(basis1[2])
    behind = placed0 * scale(basis0[0])
    for i in range(2):
        send_fwd[0, i] = ahead[i * size : (i + 1) * size]
        send_back[i] = behind[i * size : (i + 1) * size]

    @pl.when(has_after)
    def _():
        for i in range(2):
            to_after(0, i).start()

    @pl.when(has_before)
    def _():
        for i in range(2):
            to_before(i).start()

    for k in range(2):
        own = placed0 * scale(basis0[1 + k]) + placed1 * scale(basis1[k])
        mine[s, k] = own[:size]
        send_side[k] = own[size:]
    side.start()

    for copy in small[3:]:
        copy.wait()
    remote(send_side, mine.at[1 - s], side_sem.at[0], side_sem.at[1], (d, 1 - s)).wait_recv()

    @pl.when(has_after)
    def _():
        for i in range(2):
            remote(
                send_back.at[i],
                recv_back.at[i],
                back_send_sem.at[i],
                back_recv_sem.at[i],
                (d + 1, i),
            ).wait_recv()

    @pl.when(has_before)
    def _():
        for i in range(2):
            for k in range(2):
                remote(
                    send_fwd.at[k, i],
                    recv_fwd.at[k, i],
                    fwd_send_sem.at[k, i],
                    fwd_recv_sem.at[k, i],
                    (d - 1, i),
                ).wait_recv()

    for i in range(2):
        total_ref[0, i] = mine[i, 0] + recv_fwd[0, i]
        total_ref[1, i] = mine[i, 1] + recv_fwd[1, i] + recv_back[i]

    side.wait_send()

    @pl.when(has_after)
    def _():
        for i in range(2):
            to_after(1, i).wait_send()
            to_after(0, i).wait_send()

    @pl.when(has_before)
    def _():
        for i in range(2):
            to_before(i).wait_send()


def spread_kernel(total_ref, spread, pick, hess_hbm, grad_hbm, hess, grad, sem):
    cap = 2 * total_ref.shape[2] // 3
    half = cap // 2
    lane = lax.broadcasted_iota(jnp.int32, (1, 128), 1)
    copies = []

    def store(src, dst):
        copies.append(pltpu.make_async_copy(src, dst, sem.at[len(copies)]))
        copies[-1].start()

    for k in range(2):
        wide = []
        for i in range(2):
            tail = total_ref[k, i, cap:]
            for j in range(2):
                kept = jnp.where((lane < 64) == (j == 0), tail, 0.0)
                wide.append(
                    jnp.concatenate([total_ref[k, i, j * half : (j + 1) * half], kept], axis=1)
                )
        both = jnp.concatenate(split2(jnp.concatenate(wide, axis=0)), axis=0)
        slots = 2 * cap
        spread_both = jnp.dot(both, spread[...], preferred_element_type=F32)
        hess[k] = spread_both[:slots] + spread_both[slots:]
        store(hess.at[k], hess_hbm.at[k])
        grad[k] = dot_nt(pick[...], both[:slots]) + dot_nt(pick[...], both[slots:])
        store(grad.at[k], grad_hbm.at[k])
    for copy in copies:
        copy.wait()


def per_device(n, n_space, image_gradient, residual, phase, counts, owner):
    steps, bricks, comps, voxels = image_gradient.shape
    cap = 3 * bricks // (2 * n_space)
    slots = n_space * cap
    size = cap + cap // 2
    hessian_lanes, gradient_lanes = spread_tables()
    hbm = pl.BlockSpec(memory_space=pltpu.HBM)
    vmem = pl.BlockSpec(memory_space=pltpu.VMEM)
    chunks = max(map(len, CHUNKS))
    dma = pltpu.SemaphoreType.DMA
    totals, spread, pick = pl.pallas_call(
        functools.partial(kernel, n),
        out_shape=(
            jax.ShapeDtypeStruct((steps, 2, size, 128), F32),
            jax.ShapeDtypeStruct((256, PATCH), BF16),
            jax.ShapeDtypeStruct((DOFS, 256), BF16),
        ),
        in_specs=[hbm] * 8,
        out_specs=(vmem, vmem, vmem),
        scratch_shapes=[
            pltpu.VMEM((steps, comps, bricks, voxels), BF16),
            pltpu.VMEM((steps, bricks, voxels), BF16),
            pltpu.SMEM((steps,), F32),
            pltpu.VMEM((1, bricks), jnp.int32),
            pltpu.VMEM((1, bricks), jnp.int32),
            pltpu.VMEM((voxels, 256), BF16),
            pltpu.VMEM((bricks, voxels), BF16),
            pltpu.VMEM((2, 2, size, 128), F32),
            pltpu.VMEM((2, size, 128), F32),
            pltpu.VMEM((2, size, 128), F32),
            pltpu.VMEM((2, 2, size, 128), F32),
            pltpu.VMEM((2, size, 128), F32),
            pltpu.VMEM((2, 2, size, 128), F32),
            dma((3, 2, chunks)),
            dma((5,)),
            dma((2, 2)),
            dma((2, 2)),
            dma((2,)),
            dma((2,)),
            dma((2,)),
        ],
        compiler_params=pltpu.CompilerParams(
            collective_id=0, has_side_effects=True, vmem_limit_bytes=40 << 20
        ),
    )(
        *[
            pltpu.with_memory_space_constraint(x, pltpu.HBM)
            for x in (
                jnp.transpose(image_gradient, (0, 2, 1, 3)),
                residual,
                phase,
                counts.reshape(1, bricks),
                owner.reshape(1, bricks),
                jnp.asarray(moment_table()),
                jnp.asarray(hessian_lanes),
                jnp.asarray(gradient_lanes),
            )
        ]
    )
    hess, grad = pl.pallas_call(
        spread_kernel,
        out_shape=(
            jax.ShapeDtypeStruct((steps, slots, PATCH), F32),
            jax.ShapeDtypeStruct((steps, DOFS, slots), F32),
        ),
        in_specs=[vmem] * 3,
        out_specs=(hbm, hbm),
        scratch_shapes=[
            pltpu.VMEM((steps, slots, PATCH), F32),
            pltpu.VMEM((steps, DOFS, slots), F32),
            dma((2 * steps,)),
        ],
        compiler_params=pltpu.CompilerParams(vmem_limit_bytes=16 << 20),
    )(totals, spread, pick)
    return hess, jnp.transpose(grad, (0, 2, 1))


def solution(mesh):
    in_specs = (
        P("tm", "space", None, None),
        P("tm", "space", None),
        P("tm"),
        P("space"),
        P("space", None),
    )
    out_specs = (P("tm", "space", None), P("tm", "space", None))
    return jax.shard_map(
        functools.partial(per_device, mesh.shape["tm"], mesh.shape["space"]),
        mesh=mesh,
        in_specs=in_specs,
        out_specs=out_specs,
        check_vma=False,
    )
```

```python
import functools

import jax
import jax.numpy as jnp
import numpy as np
from jax import lax
from jax.experimental import pallas as pl
from jax.experimental.pallas import tpu as pltpu
from jax.sharding import PartitionSpec as P

EDGE = 16
COMPS = 3
NODES = 8
DOFS = NODES * COMPS
PATCH = DOFS * DOFS
MOMENTS = 27
PAIRS = ((0, 0), (0, 1), (0, 2), (1, 1), (1, 2), (2, 2))
TILE = 256
BLOCK = 32
CHUNKS = ((2048, 2048), (2048, 2048))
EARLY = 2
AHEAD = 6
MESH = pl.DeviceIdType.MESH
F32 = jnp.float32
BF16 = jnp.bfloat16


def two_terms(table):
    high = table.astype(BF16)
    return high, (table - high.astype(np.float64)).astype(BF16)


def moment_table():
    voxel = np.arange(EDGE**3)
    axes = [voxel // (EDGE * EDGE), voxel // EDGE % EDGE, voxel % EDGE]
    u = [(axis + 0.5) / EDGE for axis in axes]
    quads = [((1 - x) ** 2, x * (1 - x), x * x) for x in u]
    lines = [(1 - x, x) for x in u]
    exact = np.zeros((EDGE**3, 2 * BLOCK))
    for block in range(2):
        for m in range(MOMENTS):
            exact[:, BLOCK * block + m] = quads[0][m // 9] * quads[1][m // 3 % 3] * quads[2][m % 3]
        for i in range(4):
            a = 4 * block + i
            exact[:, BLOCK * block + MOMENTS + i] = (
                lines[0][a >> 2 & 1] * lines[1][a >> 1 & 1] * lines[2][a & 1]
            )
    return np.concatenate(two_terms(exact), axis=1)


def spread_tables():
    hessian = np.zeros((256, PATCH), np.float32)
    gradient = np.zeros((DOFS, 256), np.float32)
    for a in range(NODES):
        for c in range(COMPS):
            gradient[COMPS * a + c, BLOCK * (2 * c + a // 4) + MOMENTS + a % 4] = 1.0
            for b in range(NODES):
                for e in range(COMPS):
                    pair = PAIRS.index((min(c, e), max(c, e)))
                    bits = [(a >> s & 1) + (b >> s & 1) for s in (2, 1, 0)]
                    moment = bits[0] * 9 + bits[1] * 3 + bits[2]
                    hessian[BLOCK * pair + moment, (COMPS * a + c) * DOFS + COMPS * b + e] = 1.0
    hessian[192:] = hessian[128:192]
    gradient[:, 192:] = gradient[:, 128:192]
    return hessian.astype(BF16), gradient.astype(BF16)


def split3(x):
    first = x.astype(BF16)
    rest = x - first.astype(F32)
    second = rest.astype(BF16)
    return first, second, (rest - second.astype(F32)).astype(BF16)


def split2(x):
    first = x.astype(BF16)
    return first, (x - first.astype(F32)).astype(BF16)


def dot_nt(a, b):
    return lax.dot_general(a, b, (((1,), (1,)), ((), ())), preferred_element_type=F32)


def kernel(
    n,
    image_hbm,
    resid_hbm,
    phase_hbm,
    counts_hbm,
    owner_hbm,
    table_hbm,
    spread_hbm,
    pick_hbm,
    total_ref,
    spread,
    pick,
    image,
    resid,
    phase,
    counts,
    owner,
    table,
    mask,
    send_fwd,
    send_back,
    send_side,
    recv_fwd,
    recv_back,
    mine,
    load_sem,
    small_sem,
    fwd_send_sem,
    fwd_recv_sem,
    back_send_sem,
    back_recv_sem,
    side_sem,
):
    bricks, voxels = resid.shape[1], resid.shape[2]
    cap = 2 * mine.shape[2] // 3
    half = cap // 2
    d = lax.axis_index("tm")
    s = lax.axis_index("space")
    has_before = d > 0
    has_after = d < n - 1

    small = [
        pltpu.make_async_copy(counts_hbm, counts, small_sem.at[0]),
        pltpu.make_async_copy(owner_hbm, owner, small_sem.at[1]),
        pltpu.make_async_copy(phase_hbm, phase, small_sem.at[2]),
        pltpu.make_async_copy(spread_hbm, spread, small_sem.at[3]),
        pltpu.make_async_copy(pick_hbm, pick, small_sem.at[4]),
    ]
    small[0].start()
    loads = {}
    for t in (1, 0):
        for k, size in enumerate(CHUNKS[t]):
            span = pl.ds(sum(CHUNKS[t][:k]), size)
            loads[t, k] = [
                pltpu.make_async_copy(
                    image_hbm.at[t, :, :, span], image.at[t, :, :, span], load_sem.at[0, t, k]
                ),
                pltpu.make_async_copy(
                    resid_hbm.at[t, :, span], resid.at[t, :, span], load_sem.at[1, t, k]
                ),
            ]
            if t == 1:
                loads[t, k].append(
                    pltpu.make_async_copy(
                        table_hbm.at[span], table.at[span], load_sem.at[2, t, k]
                    )
                )
            if t == 1 and k < EARLY:
                for copy in loads[t, k]:
                    copy.start()
            if t == 1 and k == 0:
                for copy in small[1:3]:
                    copy.start()

    barrier = pltpu.get_barrier_semaphore()

    def greet(where):
        pl.semaphore_signal(barrier, inc=1, device_id=where, device_id_type=MESH)

    greet((d, 1 - s))

    @pl.when(has_before)
    def _():
        greet((d - 1, 0))
        greet((d - 1, 1))

    @pl.when(has_after)
    def _():
        greet((d + 1, 0))
        greet((d + 1, 1))

    for copy in small[:3]:
        copy.wait()
    square = lax.broadcasted_iota(jnp.int32, (bricks, bricks), 0) == lax.broadcasted_iota(
        jnp.int32, (bricks, bricks), 1
    )

    def column(row):
        return jnp.sum(
            jnp.where(square, jnp.broadcast_to(row, (bricks, bricks)), 0.0), axis=1, keepdims=True
        )

    count = jnp.broadcast_to(column(counts[...].astype(F32)), (bricks, TILE))
    voxel = lax.broadcasted_iota(jnp.int32, (bricks, TILE), 1).astype(F32)
    lane = lax.broadcasted_iota(jnp.int32, (1, 128), 1)
    spare = lane % BLOCK >= MOMENTS

    def add_tiles(t, accs, begin, end):
        for tile in range(begin, end):
            unit, staging = tile % 2, tile // 2 % 2
            span = slice(tile * TILE, (tile + 1) * TILE)
            part = table[span, :]
            pltpu.matmul_push_rhs(jnp.concatenate([part, part], axis=1), staging, unit)
            if t == 1:
                mask[:, span] = jnp.where(voxel < count - tile * TILE, 1.0, 0.0).astype(BF16)
            valid = mask[:, span]
            g = [image[t, c, :, span] * valid for c in range(COMPS)]
            r = resid[t, :, span]
            products = [g[c] * g[e] for c, e in PAIRS] + [g[c] * r for c in range(COMPS)]
            for q, product in enumerate(products):
                pltpu.matmul_acc_lhs(accs[9 * unit + q], product, staging if q == 0 else None)

    def pop_sums(accs):
        found = []
        for q in range(9):
            both = (pltpu.matmul_pop(accs[q]) + pltpu.matmul_pop(accs[9 + q]))[:, :128]
            found.append(both + pltpu.roll(both, 64, 1))
        return found

    def arranged(found):
        first = jnp.where(lane < 2 * BLOCK, found[6], found[7])
        for q in range(4):
            first = jnp.where(jnp.logical_and(lane // BLOCK == q, jnp.logical_not(spare)), found[q], first)
        second = jnp.where(spare, found[8], jnp.where(lane // BLOCK % 2 == 0, found[4], found[5]))
        return jnp.concatenate([first, second], axis=1)


    def slot_table():
        who = owner[...].astype(F32)
        who_column = column(who)
        earlier = lax.broadcasted_iota(jnp.int32, (bricks, bricks), 0) < lax.broadcasted_iota(
            jnp.int32, (bricks, bricks), 1
        )
        ones_before = jnp.sum(jnp.where(earlier, who_column, 0.0), axis=0, keepdims=True)
        place = lax.broadcasted_iota(jnp.int32, (1, bricks), 1).astype(F32)
        rank = jnp.where(who > 0.5, ones_before, place - ones_before)
        mine_first = jnp.where(s == 0, who, 1.0 - who)
        target = mine_first * cap + rank
        slot = lax.broadcasted_iota(jnp.int32, (2 * cap, bricks), 0).astype(F32)
        hit = jnp.where(slot == jnp.broadcast_to(target, (2 * cap, bricks)), 1.0, 0.0)
        hit = hit.astype(BF16)
        return jnp.concatenate([hit, hit, hit, jnp.zeros_like(hit)], axis=1)

    def placed(x, hits, acc):
        pltpu.matmul_push_rhs(
            jnp.concatenate([*split3(x), jnp.zeros(x.shape, BF16)], axis=0), 0, 0
        )
        pltpu.matmul_acc_lhs(acc, hits, 0)
        rows = pltpu.matmul_pop(acc)
        out = []
        for i in range(2):
            part = rows[i * cap : (i + 1) * cap]
            out.append(part[:, :128])
            out.append(jnp.where(lane < 64, part[:half, 128:], part[half:, 128:]))
        return jnp.concatenate(out, axis=0)

    first = jnp.where(has_before, 0.0, 1.0)
    last = jnp.where(has_after, 0.0, 1.0)

    def weights(t):
        u = phase[t]
        v = 1.0 - u
        return (
            v * v * v * (1.0 / 6.0),
            (3.0 * u * u * u - 6.0 * u * u + 4.0) * (1.0 / 6.0),
            (-3.0 * u * u * u + 3.0 * u * u + 3.0 * u + 1.0) * (1.0 / 6.0),
            u * u * u * (1.0 / 6.0),
        )

    w = weights(0)
    basis0 = (w[0] * (1.0 - first), w[1] + first * w[0], w[2] + last * w[3], w[3] * (1.0 - last))
    w = weights(1)
    basis1 = (w[0], w[1] + last * (w[2] + w[3]), w[2] * (1.0 - last), w[3] * (1.0 - last))
    size = cap + half

    def scale(b):
        return jnp.where(spare, b, b * b)

    def remote(src, dst, send_sem, recv_sem, where):
        return pltpu.make_async_remote_copy(
            src_ref=src,
            dst_ref=dst,
            send_sem=send_sem,
            recv_sem=recv_sem,
            device_id=where,
            device_id_type=MESH,
        )

    cores = (s, 1 - s)

    def to_after(k, i):
        return remote(
            send_fwd.at[k, i],
            recv_fwd.at[k, s],
            fwd_send_sem.at[k, i],
            fwd_recv_sem.at[k, s],
            (d + 1, cores[i]),
        )

    def to_before(i):
        return remote(
            send_back.at[i],
            recv_back.at[s],
            back_send_sem.at[i],
            back_recv_sem.at[s],
            (d - 1, cores[i]),
        )

    side = remote(send_side, mine.at[s], side_sem.at[0], side_sem.at[1], (d, 1 - s))

    def send_second(placed1):
        ahead = placed1 * scale(basis1[3])
        for i in range(2):
            send_fwd[1, i] = ahead[i * size : (i + 1) * size]

        pl.semaphore_wait(barrier, 1 + 2 * has_before.astype(jnp.int32) + 2 * has_after.astype(jnp.int32))

        @pl.when(jnp.logical_not(has_before))
        def _():
            recv_fwd[...] = jnp.zeros(recv_fwd.shape, F32)

        @pl.when(has_after)
        def _():
            for i in range(2):
                to_after(1, i).start()

        @pl.when(jnp.logical_not(has_after))
        def _():
            recv_back[...] = jnp.zeros(recv_back.shape, F32)

    tiles = voxels // TILE

    def second_step(*accs):
        done = 0
        for k, voxel_count in enumerate(CHUNKS[1]):
            for copy in loads[1, k]:
                copy.wait()
            if k == 0:
                for later in [(1, j) for j in range(EARLY, len(CHUNKS[1]))] + [(0, j) for j in range(len(CHUNKS[0]))]:
                    for copy in loads[later]:
                        copy.start()
                for copy in small[3:]:
                    copy.start()
            add_tiles(1, accs, done, done + voxel_count // TILE)
            done += voxel_count // TILE
            if k == 0:
                hits = slot_table()
        return hits, pop_sums(accs)

    def first_step(place_acc, *accs):
        for k in range(len(CHUNKS[0])):
            for copy in loads[0, k]:
                copy.wait()
        add_tiles(0, accs, 0, AHEAD)
        placed1 = placed(arranged(found), hits, place_acc)
        send_second(placed1)
        add_tiles(0, accs, AHEAD, tiles)
        return placed1, placed(arranged(pop_sums(accs)), hits, place_acc)

    sums_acc = [pltpu.ACC(unit)((bricks, 256), F32) for unit in range(2) for _ in range(9)]
    hits, found = pl.run_scoped(second_step, *sums_acc)
    placed1, placed0 = pl.run_scoped(first_step, pltpu.ACC(0)((2 * cap, 256), F32), *sums_acc)
    ahead = placed0 * scale(basis0[3]) + placed1 * scale(basis1[2])
    for i in range(2):
        send_fwd[0, i] = ahead[i * size : (i + 1) * size]

    @pl.when(has_after)
    def _():
        for i in range(2):
            to_after(0, i).start()

    behind = placed0 * scale(basis0[0])
    for i in range(2):
        send_back[i] = behind[i * size : (i + 1) * size]

    @pl.when(has_before)
    def _():
        for i in range(2):
            to_before(i).start()

    for k in range(2):
        own = placed0 * scale(basis0[1 + k]) + placed1 * scale(basis1[k])
        mine[s, k] = own[:size]
        send_side[k] = own[size:]
    side.start()

    for copy in small[3:]:
        copy.wait()
    remote(send_side, mine.at[1 - s], side_sem.at[0], side_sem.at[1], (d, 1 - s)).wait_recv()

    @pl.when(has_after)
    def _():
        for i in range(2):
            remote(
                send_back.at[i],
                recv_back.at[i],
                back_send_sem.at[i],
                back_recv_sem.at[i],
                (d + 1, i),
            ).wait_recv()

    @pl.when(has_before)
    def _():
        for i in range(2):
            for k in range(2):
                remote(
                    send_fwd.at[k, i],
                    recv_fwd.at[k, i],
                    fwd_send_sem.at[k, i],
                    fwd_recv_sem.at[k, i],
                    (d - 1, i),
                ).wait_recv()

    for i in range(2):
        total_ref[0, i] = mine[i, 0] + recv_fwd[0, i]
        total_ref[1, i] = mine[i, 1] + recv_fwd[1, i] + recv_back[i]

    side.wait_send()

    @pl.when(has_after)
    def _():
        for i in range(2):
            to_after(1, i).wait_send()
            to_after(0, i).wait_send()

    @pl.when(has_before)
    def _():
        for i in range(2):
            to_before(i).wait_send()


def spread_kernel(total_ref, spread, pick, hess_hbm, grad_hbm, hess, grad, sem):
    cap = 2 * total_ref.shape[2] // 3
    half = cap // 2
    lane = lax.broadcasted_iota(jnp.int32, (1, 128), 1)
    copies = []

    def store(src, dst):
        copies.append(pltpu.make_async_copy(src, dst, sem.at[len(copies)]))
        copies[-1].start()

    for k in range(2):
        wide = []
        for i in range(2):
            tail = total_ref[k, i, cap:]
            for j in range(2):
                kept = jnp.where((lane < 64) == (j == 0), tail, 0.0)
                wide.append(
                    jnp.concatenate([total_ref[k, i, j * half : (j + 1) * half], kept], axis=1)
                )
        both = jnp.concatenate(split2(jnp.concatenate(wide, axis=0)), axis=0)
        slots = 2 * cap
        spread_both = jnp.dot(both, spread[...], preferred_element_type=F32)
        hess[k] = spread_both[:slots] + spread_both[slots:]
        store(hess.at[k], hess_hbm.at[k])
        grad[k] = dot_nt(pick[...], both[:slots]) + dot_nt(pick[...], both[slots:])
        store(grad.at[k], grad_hbm.at[k])
    for copy in copies:
        copy.wait()


def per_device(n, n_space, image_gradient, residual, phase, counts, owner):
    steps, bricks, comps, voxels = image_gradient.shape
    cap = 3 * bricks // (2 * n_space)
    slots = n_space * cap
    size = cap + cap // 2
    hessian_lanes, gradient_lanes = spread_tables()
    hbm = pl.BlockSpec(memory_space=pltpu.HBM)
    vmem = pl.BlockSpec(memory_space=pltpu.VMEM)
    chunks = max(map(len, CHUNKS))
    dma = pltpu.SemaphoreType.DMA
    totals, spread, pick = pl.pallas_call(
        functools.partial(kernel, n),
        out_shape=(
            jax.ShapeDtypeStruct((steps, 2, size, 128), F32),
            jax.ShapeDtypeStruct((256, PATCH), BF16),
            jax.ShapeDtypeStruct((DOFS, 256), BF16),
        ),
        in_specs=[hbm] * 8,
        out_specs=(vmem, vmem, vmem),
        scratch_shapes=[
            pltpu.VMEM((steps, comps, bricks, voxels), BF16),
            pltpu.VMEM((steps, bricks, voxels), BF16),
            pltpu.SMEM((steps,), F32),
            pltpu.VMEM((1, bricks), jnp.int32),
            pltpu.VMEM((1, bricks), jnp.int32),
            pltpu.VMEM((voxels, 128), BF16),
            pltpu.VMEM((bricks, voxels), BF16),
            pltpu.VMEM((2, 2, size, 128), F32),
            pltpu.VMEM((2, size, 128), F32),
            pltpu.VMEM((2, size, 128), F32),
            pltpu.VMEM((2, 2, size, 128), F32),
            pltpu.VMEM((2, size, 128), F32),
            pltpu.VMEM((2, 2, size, 128), F32),
            dma((3, 2, chunks)),
            dma((5,)),
            dma((2, 2)),
            dma((2, 2)),
            dma((2,)),
            dma((2,)),
            dma((2,)),
        ],
        compiler_params=pltpu.CompilerParams(
            collective_id=0, has_side_effects=True, vmem_limit_bytes=40 << 20
        ),
    )(
        *[
            pltpu.with_memory_space_constraint(x, pltpu.HBM)
            for x in (
                jnp.transpose(image_gradient, (0, 2, 1, 3)),
                residual,
                phase,
                counts.reshape(1, bricks),
                owner.reshape(1, bricks),
                jnp.asarray(moment_table()),
                jnp.asarray(hessian_lanes),
                jnp.asarray(gradient_lanes),
            )
        ]
    )
    hess, grad = pl.pallas_call(
        spread_kernel,
        out_shape=(
            jax.ShapeDtypeStruct((steps, slots, PATCH), F32),
            jax.ShapeDtypeStruct((steps, DOFS, slots), F32),
        ),
        in_specs=[vmem] * 3,
        out_specs=(hbm, hbm),
        scratch_shapes=[
            pltpu.VMEM((steps, slots, PATCH), F32),
            pltpu.VMEM((steps, DOFS, slots), F32),
            dma((2 * steps,)),
        ],
        compiler_params=pltpu.CompilerParams(vmem_limit_bytes=16 << 20),
    )(totals, spread, pick)
    return hess, jnp.transpose(grad, (0, 2, 1))


def solution(mesh):
    in_specs = (
        P("tm", "space", None, None),
        P("tm", "space", None),
        P("tm"),
        P("space"),
        P("space", None),
    )
    out_specs = (P("tm", "space", None), P("tm", "space", None))
    return jax.shard_map(
        functools.partial(per_device, mesh.shape["tm"], mesh.shape["space"]),
        mesh=mesh,
        in_specs=in_specs,
        out_specs=out_specs,
        check_vma=False,
    )
```

```python
import functools

import jax
import jax.numpy as jnp
import numpy as np
from jax import lax
from jax.experimental import pallas as pl
from jax.experimental.pallas import tpu as pltpu
from jax.sharding import PartitionSpec as P

EDGE = 16
COMPS = 3
NODES = 8
DOFS = NODES * COMPS
PATCH = DOFS * DOFS
MOMENTS = 27
PAIRS = ((0, 0), (0, 1), (0, 2), (1, 1), (1, 2), (2, 2))
TILE = 256
BLOCK = 32
CHUNKS = ((2048, 2048), (1024, 3072))
EARLY = 2
AHEAD = 6
MESH = pl.DeviceIdType.MESH
F32 = jnp.float32
BF16 = jnp.bfloat16


def two_terms(table):
    high = table.astype(BF16)
    return high, (table - high.astype(np.float64)).astype(BF16)


def moment_table():
    voxel = np.arange(EDGE**3)
    axes = [voxel // (EDGE * EDGE), voxel // EDGE % EDGE, voxel % EDGE]
    u = [(axis + 0.5) / EDGE for axis in axes]
    quads = [((1 - x) ** 2, x * (1 - x), x * x) for x in u]
    lines = [(1 - x, x) for x in u]
    exact = np.zeros((EDGE**3, 2 * BLOCK))
    for block in range(2):
        for m in range(MOMENTS):
            exact[:, BLOCK * block + m] = quads[0][m // 9] * quads[1][m // 3 % 3] * quads[2][m % 3]
        for i in range(4):
            a = 4 * block + i
            exact[:, BLOCK * block + MOMENTS + i] = (
                lines[0][a >> 2 & 1] * lines[1][a >> 1 & 1] * lines[2][a & 1]
            )
    return np.concatenate(two_terms(exact), axis=1)


def spread_tables():
    hessian = np.zeros((256, PATCH), np.float32)
    gradient = np.zeros((DOFS, 256), np.float32)
    for a in range(NODES):
        for c in range(COMPS):
            gradient[COMPS * a + c, BLOCK * (2 * c + a // 4) + MOMENTS + a % 4] = 1.0
            for b in range(NODES):
                for e in range(COMPS):
                    pair = PAIRS.index((min(c, e), max(c, e)))
                    bits = [(a >> s & 1) + (b >> s & 1) for s in (2, 1, 0)]
                    moment = bits[0] * 9 + bits[1] * 3 + bits[2]
                    hessian[BLOCK * pair + moment, (COMPS * a + c) * DOFS + COMPS * b + e] = 1.0
    hessian[192:] = hessian[128:192]
    gradient[:, 192:] = gradient[:, 128:192]
    return hessian.astype(BF16), gradient.astype(BF16)


def split3(x):
    first = x.astype(BF16)
    rest = x - first.astype(F32)
    second = rest.astype(BF16)
    return first, second, (rest - second.astype(F32)).astype(BF16)


def split2(x):
    first = x.astype(BF16)
    return first, (x - first.astype(F32)).astype(BF16)


def dot_nt(a, b):
    return lax.dot_general(a, b, (((1,), (1,)), ((), ())), preferred_element_type=F32)


def kernel(
    n,
    image_hbm,
    resid_hbm,
    phase_hbm,
    counts_hbm,
    owner_hbm,
    table_hbm,
    spread_hbm,
    pick_hbm,
    total_ref,
    spread,
    pick,
    image,
    resid,
    phase,
    counts,
    owner,
    table,
    mask,
    send_fwd,
    send_back,
    send_side,
    recv_fwd,
    recv_back,
    mine,
    load_sem,
    small_sem,
    fwd_send_sem,
    fwd_recv_sem,
    back_send_sem,
    back_recv_sem,
    side_sem,
):
    bricks, voxels = resid.shape[1], resid.shape[2]
    cap = 2 * mine.shape[2] // 3
    half = cap // 2
    d = lax.axis_index("tm")
    s = lax.axis_index("space")
    has_before = d > 0
    has_after = d < n - 1

    small = [
        pltpu.make_async_copy(counts_hbm, counts, small_sem.at[0]),
        pltpu.make_async_copy(owner_hbm, owner, small_sem.at[1]),
        pltpu.make_async_copy(phase_hbm, phase, small_sem.at[2]),
        pltpu.make_async_copy(spread_hbm, spread, small_sem.at[3]),
        pltpu.make_async_copy(pick_hbm, pick, small_sem.at[4]),
    ]
    small[0].start()
    loads = {}
    for t in (1, 0):
        for k, size in enumerate(CHUNKS[t]):
            span = pl.ds(sum(CHUNKS[t][:k]), size)
            loads[t, k] = [
                pltpu.make_async_copy(
                    image_hbm.at[t, :, :, span], image.at[t, :, :, span], load_sem.at[0, t, k]
                ),
                pltpu.make_async_copy(
                    resid_hbm.at[t, :, span], resid.at[t, :, span], load_sem.at[1, t, k]
                ),
            ]
            if t == 1:
                loads[t, k].append(
                    pltpu.make_async_copy(
                        table_hbm.at[span], table.at[span], load_sem.at[2, t, k]
                    )
                )
            if t == 1 and k < EARLY:
                for copy in loads[t, k]:
                    copy.start()
            if t == 1 and k == 0:
                for copy in small[1:3]:
                    copy.start()

    barrier = pltpu.get_barrier_semaphore()

    def greet(where):
        pl.semaphore_signal(barrier, inc=1, device_id=where, device_id_type=MESH)

    greet((d, 1 - s))

    @pl.when(has_before)
    def _():
        greet((d - 1, 0))
        greet((d - 1, 1))

    @pl.when(has_after)
    def _():
        greet((d + 1, 0))
        greet((d + 1, 1))

    for copy in small[:3]:
        copy.wait()
    square = lax.broadcasted_iota(jnp.int32, (bricks, bricks), 0) == lax.broadcasted_iota(
        jnp.int32, (bricks, bricks), 1
    )

    def column(row):
        return jnp.sum(
            jnp.where(square, jnp.broadcast_to(row, (bricks, bricks)), 0.0), axis=1, keepdims=True
        )

    count = jnp.broadcast_to(column(counts[...].astype(F32)), (bricks, TILE))
    voxel = lax.broadcasted_iota(jnp.int32, (bricks, TILE), 1).astype(F32)
    lane = lax.broadcasted_iota(jnp.int32, (1, 128), 1)
    spare = lane % BLOCK >= MOMENTS

    def add_tiles(t, accs, begin, end):
        for tile in range(begin, end):
            unit, staging = tile % 2, tile // 2 % 2
            span = slice(tile * TILE, (tile + 1) * TILE)
            part = table[span, :]
            pltpu.matmul_push_rhs(jnp.concatenate([part, part], axis=1), staging, unit)
            if t == 1:
                mask[:, span] = jnp.where(voxel < count - tile * TILE, 1.0, 0.0).astype(BF16)
            valid = mask[:, span]
            g = [image[t, c, :, span] * valid for c in range(COMPS)]
            r = resid[t, :, span]
            products = [g[c] * g[e] for c, e in PAIRS] + [g[c] * r for c in range(COMPS)]
            for q, product in enumerate(products):
                pltpu.matmul_acc_lhs(accs[9 * unit + q], product, staging if q == 0 else None)

    def pop_sums(accs):
        return [
            (pltpu.matmul_pop(accs[q]) + pltpu.matmul_pop(accs[9 + q]))[:, :128] for q in range(9)
        ]

    def arranged(found):
        twos = []
        for c in range(COMPS):
            two = jnp.where(lane // BLOCK % 2 == 0, found[2 * c], found[2 * c + 1])
            two = jnp.where(spare, found[6 + c], two)
            twos.append(two + pltpu.roll(two, 64, 1))
        first = jnp.where(lane < 64, twos[0], twos[1])
        second = twos[2]
        return jnp.concatenate([first, second], axis=1)


    def slot_table():
        who = owner[...].astype(F32)
        who_column = column(who)
        earlier = lax.broadcasted_iota(jnp.int32, (bricks, bricks), 0) < lax.broadcasted_iota(
            jnp.int32, (bricks, bricks), 1
        )
        ones_before = jnp.sum(jnp.where(earlier, who_column, 0.0), axis=0, keepdims=True)
        place = lax.broadcasted_iota(jnp.int32, (1, bricks), 1).astype(F32)
        rank = jnp.where(who > 0.5, ones_before, place - ones_before)
        mine_first = jnp.where(s == 0, who, 1.0 - who)
        target = mine_first * cap + rank
        slot = lax.broadcasted_iota(jnp.int32, (2 * cap, bricks), 0).astype(F32)
        hit = jnp.where(slot == jnp.broadcast_to(target, (2 * cap, bricks)), 1.0, 0.0)
        hit = hit.astype(BF16)
        return jnp.concatenate([hit, hit, hit, jnp.zeros_like(hit)], axis=1)

    def start_place(x, hits, acc):
        pltpu.matmul_push_rhs(
            jnp.concatenate([*split3(x), jnp.zeros(x.shape, BF16)], axis=0), 0, 0
        )
        pltpu.matmul_acc_lhs(acc, hits, 0)

    def placed(acc):
        rows = pltpu.matmul_pop(acc)
        out = []
        for i in range(2):
            part = rows[i * cap : (i + 1) * cap]
            out.append(part[:, :128])
            out.append(jnp.where(lane < 64, part[:half, 128:], part[half:, 128:]))
        return jnp.concatenate(out, axis=0)

    first = jnp.where(has_before, 0.0, 1.0)
    last = jnp.where(has_after, 0.0, 1.0)

    def weights(t):
        u = phase[t]
        v = 1.0 - u
        return (
            v * v * v * (1.0 / 6.0),
            (3.0 * u * u * u - 6.0 * u * u + 4.0) * (1.0 / 6.0),
            (-3.0 * u * u * u + 3.0 * u * u + 3.0 * u + 1.0) * (1.0 / 6.0),
            u * u * u * (1.0 / 6.0),
        )

    w = weights(0)
    basis0 = (w[0] * (1.0 - first), w[1] + first * w[0], w[2] + last * w[3], w[3] * (1.0 - last))
    w = weights(1)
    basis1 = (w[0], w[1] + last * (w[2] + w[3]), w[2] * (1.0 - last), w[3] * (1.0 - last))
    size = cap + half

    def scale(b):
        return jnp.where(spare, b, b * b)

    def remote(src, dst, send_sem, recv_sem, where):
        return pltpu.make_async_remote_copy(
            src_ref=src,
            dst_ref=dst,
            send_sem=send_sem,
            recv_sem=recv_sem,
            device_id=where,
            device_id_type=MESH,
        )

    cores = (s, 1 - s)

    def to_after(k, i):
        return remote(
            send_fwd.at[k, i],
            recv_fwd.at[k, s],
            fwd_send_sem.at[k, i],
            fwd_recv_sem.at[k, s],
            (d + 1, cores[i]),
        )

    def to_before(i):
        return remote(
            send_back.at[i],
            recv_back.at[s],
            back_send_sem.at[i],
            back_recv_sem.at[s],
            (d - 1, cores[i]),
        )

    side = remote(send_side, mine.at[s], side_sem.at[0], side_sem.at[1], (d, 1 - s))

    def send_second(placed1):
        ahead = placed1 * scale(basis1[3])
        for i in range(2):
            send_fwd[1, i] = ahead[i * size : (i + 1) * size]

        pl.semaphore_wait(barrier, 1 + 2 * has_before.astype(jnp.int32) + 2 * has_after.astype(jnp.int32))

        @pl.when(jnp.logical_not(has_before))
        def _():
            recv_fwd[...] = jnp.zeros(recv_fwd.shape, F32)

        @pl.when(has_after)
        def _():
            for i in range(2):
                to_after(1, i).start()

        @pl.when(jnp.logical_not(has_after))
        def _():
            recv_back[...] = jnp.zeros(recv_back.shape, F32)

    tiles = voxels // TILE

    def second_step(*accs):
        done = 0
        for k, voxel_count in enumerate(CHUNKS[1]):
            for copy in loads[1, k]:
                copy.wait()
            if k == 0:
                for later in [(1, j) for j in range(EARLY, len(CHUNKS[1]))] + [(0, j) for j in range(len(CHUNKS[0]))]:
                    for copy in loads[later]:
                        copy.start()
                for copy in small[3:]:
                    copy.start()
            add_tiles(1, accs, done, done + voxel_count // TILE)
            done += voxel_count // TILE
            if k == 0:
                hits = slot_table()
        return hits, pop_sums(accs)

    def first_step(place_acc, *accs):
        for k in range(len(CHUNKS[0])):
            for copy in loads[0, k]:
                copy.wait()
        add_tiles(0, accs, 0, AHEAD)
        start_place(arranged(found), hits, place_acc)
        add_tiles(0, accs, AHEAD, 2 * AHEAD)
        placed1 = placed(place_acc)
        send_second(placed1)
        add_tiles(0, accs, 2 * AHEAD, tiles)
        start_place(arranged(pop_sums(accs)), hits, place_acc)
        return placed1, placed(place_acc)

    sums_acc = [pltpu.ACC(unit)((bricks, 256), F32) for unit in range(2) for _ in range(9)]
    hits, found = pl.run_scoped(second_step, *sums_acc)
    placed1, placed0 = pl.run_scoped(first_step, pltpu.ACC(0)((2 * cap, 256), F32), *sums_acc)
    ahead = placed0 * scale(basis0[3]) + placed1 * scale(basis1[2])
    for i in range(2):
        send_fwd[0, i] = ahead[i * size : (i + 1) * size]

    @pl.when(has_after)
    def _():
        for i in range(2):
            to_after(0, i).start()

    behind = placed0 * scale(basis0[0])
    for i in range(2):
        send_back[i] = behind[i * size : (i + 1) * size]

    @pl.when(has_before)
    def _():
        for i in range(2):
            to_before(i).start()

    for k in range(2):
        own = placed0 * scale(basis0[1 + k]) + placed1 * scale(basis1[k])
        mine[s, k] = own[:size]
        send_side[k] = own[size:]
    side.start()

    for copy in small[3:]:
        copy.wait()
    remote(send_side, mine.at[1 - s], side_sem.at[0], side_sem.at[1], (d, 1 - s)).wait_recv()

    @pl.when(has_after)
    def _():
        for i in range(2):
            remote(
                send_back.at[i],
                recv_back.at[i],
                back_send_sem.at[i],
                back_recv_sem.at[i],
                (d + 1, i),
            ).wait_recv()

    @pl.when(has_before)
    def _():
        for i in range(2):
            for k in range(2):
                remote(
                    send_fwd.at[k, i],
                    recv_fwd.at[k, i],
                    fwd_send_sem.at[k, i],
                    fwd_recv_sem.at[k, i],
                    (d - 1, i),
                ).wait_recv()

    for i in range(2):
        total_ref[0, i] = mine[i, 0] + recv_fwd[0, i]
        total_ref[1, i] = mine[i, 1] + recv_fwd[1, i] + recv_back[i]

    side.wait_send()

    @pl.when(has_after)
    def _():
        for i in range(2):
            to_after(1, i).wait_send()
            to_after(0, i).wait_send()

    @pl.when(has_before)
    def _():
        for i in range(2):
            to_before(i).wait_send()


def spread_kernel(total_ref, spread, pick, hess_hbm, grad_hbm, hess, grad, sem):
    cap = 2 * total_ref.shape[2] // 3
    half = cap // 2
    lane = lax.broadcasted_iota(jnp.int32, (1, 128), 1)
    copies = []

    def store(src, dst):
        copies.append(pltpu.make_async_copy(src, dst, sem.at[len(copies)]))
        copies[-1].start()

    for k in range(2):
        wide = []
        for i in range(2):
            tail = total_ref[k, i, cap:]
            for j in range(2):
                kept = jnp.where((lane < 64) == (j == 0), tail, 0.0)
                wide.append(
                    jnp.concatenate([total_ref[k, i, j * half : (j + 1) * half], kept], axis=1)
                )
        both = jnp.concatenate(split2(jnp.concatenate(wide, axis=0)), axis=0)
        slots = 2 * cap
        spread_both = jnp.dot(both, spread[...], preferred_element_type=F32)
        hess[k] = spread_both[:slots] + spread_both[slots:]
        store(hess.at[k], hess_hbm.at[k])
        grad[k] = dot_nt(pick[...], both[:slots]) + dot_nt(pick[...], both[slots:])
        store(grad.at[k], grad_hbm.at[k])
    for copy in copies:
        copy.wait()


def per_device(n, n_space, image_gradient, residual, phase, counts, owner):
    steps, bricks, comps, voxels = image_gradient.shape
    cap = 3 * bricks // (2 * n_space)
    slots = n_space * cap
    size = cap + cap // 2
    hessian_lanes, gradient_lanes = spread_tables()
    hbm = pl.BlockSpec(memory_space=pltpu.HBM)
    vmem = pl.BlockSpec(memory_space=pltpu.VMEM)
    chunks = max(map(len, CHUNKS))
    dma = pltpu.SemaphoreType.DMA
    totals, spread, pick = pl.pallas_call(
        functools.partial(kernel, n),
        out_shape=(
            jax.ShapeDtypeStruct((steps, 2, size, 128), F32),
            jax.ShapeDtypeStruct((256, PATCH), BF16),
            jax.ShapeDtypeStruct((DOFS, 256), BF16),
        ),
        in_specs=[hbm] * 8,
        out_specs=(vmem, vmem, vmem),
        scratch_shapes=[
            pltpu.VMEM((steps, comps, bricks, voxels), BF16),
            pltpu.VMEM((steps, bricks, voxels), BF16),
            pltpu.SMEM((steps,), F32),
            pltpu.VMEM((1, bricks), jnp.int32),
            pltpu.VMEM((1, bricks), jnp.int32),
            pltpu.VMEM((voxels, 128), BF16),
            pltpu.VMEM((bricks, voxels), BF16),
            pltpu.VMEM((2, 2, size, 128), F32),
            pltpu.VMEM((2, size, 128), F32),
            pltpu.VMEM((2, size, 128), F32),
            pltpu.VMEM((2, 2, size, 128), F32),
            pltpu.VMEM((2, size, 128), F32),
            pltpu.VMEM((2, 2, size, 128), F32),
            dma((3, 2, chunks)),
            dma((5,)),
            dma((2, 2)),
            dma((2, 2)),
            dma((2,)),
            dma((2,)),
            dma((2,)),
        ],
        compiler_params=pltpu.CompilerParams(
            collective_id=0, has_side_effects=True, vmem_limit_bytes=40 << 20
        ),
    )(
        *[
            pltpu.with_memory_space_constraint(x, pltpu.HBM)
            for x in (
                jnp.transpose(image_gradient, (0, 2, 1, 3)),
                residual,
                phase,
                counts.reshape(1, bricks),
                owner.reshape(1, bricks),
                jnp.asarray(moment_table()),
                jnp.asarray(hessian_lanes),
                jnp.asarray(gradient_lanes),
            )
        ]
    )
    hess, grad = pl.pallas_call(
        spread_kernel,
        out_shape=(
            jax.ShapeDtypeStruct((steps, slots, PATCH), F32),
            jax.ShapeDtypeStruct((steps, DOFS, slots), F32),
        ),
        in_specs=[vmem] * 3,
        out_specs=(hbm, hbm),
        scratch_shapes=[
            pltpu.VMEM((steps, slots, PATCH), F32),
            pltpu.VMEM((steps, DOFS, slots), F32),
            dma((2 * steps,)),
        ],
        compiler_params=pltpu.CompilerParams(vmem_limit_bytes=16 << 20),
    )(totals, spread, pick)
    return hess, jnp.transpose(grad, (0, 2, 1))


def solution(mesh):
    in_specs = (
        P("tm", "space", None, None),
        P("tm", "space", None),
        P("tm"),
        P("space"),
        P("space", None),
    )
    out_specs = (P("tm", "space", None), P("tm", "space", None))
    return jax.shard_map(
        functools.partial(per_device, mesh.shape["tm"], mesh.shape["space"]),
        mesh=mesh,
        in_specs=in_specs,
        out_specs=out_specs,
        check_vma=False,
    )
```

```python
import functools

import jax
import jax.numpy as jnp
import numpy as np
from jax import lax
from jax.experimental import pallas as pl
from jax.experimental.pallas import tpu as pltpu
from jax.sharding import PartitionSpec as P

EDGE = 16
COMPS = 3
NODES = 8
DOFS = NODES * COMPS
PATCH = DOFS * DOFS
MOMENTS = 27
PAIRS = ((0, 0), (0, 1), (0, 2), (1, 1), (1, 2), (2, 2))
TILE = 256
BLOCK = 32
CHUNKS = ((2048, 2048), (2048, 2048))
EARLY = 2
AHEAD = 2
MESH = pl.DeviceIdType.MESH
F32 = jnp.float32
BF16 = jnp.bfloat16


def two_terms(table):
    high = table.astype(BF16)
    return high, (table - high.astype(np.float64)).astype(BF16)


def moment_table():
    voxel = np.arange(EDGE**3)
    axes = [voxel // (EDGE * EDGE), voxel // EDGE % EDGE, voxel % EDGE]
    u = [(axis + 0.5) / EDGE for axis in axes]
    quads = [((1 - x) ** 2, x * (1 - x), x * x) for x in u]
    lines = [(1 - x, x) for x in u]
    exact = np.zeros((EDGE**3, 2 * BLOCK))
    for block in range(2):
        for m in range(MOMENTS):
            exact[:, BLOCK * block + m] = quads[0][m // 9] * quads[1][m // 3 % 3] * quads[2][m % 3]
        for i in range(4):
            a = 4 * block + i
            exact[:, BLOCK * block + MOMENTS + i] = (
                lines[0][a >> 2 & 1] * lines[1][a >> 1 & 1] * lines[2][a & 1]
            )
    return np.concatenate(two_terms(exact), axis=1)


def spread_tables():
    hessian = np.zeros((256, PATCH), np.float32)
    gradient = np.zeros((DOFS, 256), np.float32)
    for a in range(NODES):
        for c in range(COMPS):
            gradient[COMPS * a + c, BLOCK * (2 * c + a // 4) + MOMENTS + a % 4] = 1.0
            for b in range(NODES):
                for e in range(COMPS):
                    pair = PAIRS.index((min(c, e), max(c, e)))
                    bits = [(a >> s & 1) + (b >> s & 1) for s in (2, 1, 0)]
                    moment = bits[0] * 9 + bits[1] * 3 + bits[2]
                    hessian[BLOCK * pair + moment, (COMPS * a + c) * DOFS + COMPS * b + e] = 1.0
    hessian[192:] = hessian[128:192]
    gradient[:, 192:] = gradient[:, 128:192]
    return hessian.astype(BF16), gradient.astype(BF16)


def split3(x):
    first = x.astype(BF16)
    rest = x - first.astype(F32)
    second = rest.astype(BF16)
    return first, second, (rest - second.astype(F32)).astype(BF16)


def split2(x):
    first = x.astype(BF16)
    return first, (x - first.astype(F32)).astype(BF16)


def dot_nt(a, b):
    return lax.dot_general(a, b, (((1,), (1,)), ((), ())), preferred_element_type=F32)


def kernel(
    n,
    image_hbm,
    resid_hbm,
    phase_hbm,
    counts_hbm,
    owner_hbm,
    table_hbm,
    spread_hbm,
    pick_hbm,
    total_ref,
    spread,
    pick,
    image,
    resid,
    phase,
    counts,
    owner,
    table,
    mask,
    send_fwd,
    send_back,
    send_side,
    recv_fwd,
    recv_back,
    mine,
    load_sem,
    small_sem,
    fwd_send_sem,
    fwd_recv_sem,
    back_send_sem,
    back_recv_sem,
    side_sem,
):
    bricks, voxels = resid.shape[1], resid.shape[2]
    cap = 2 * mine.shape[2] // 3
    half = cap // 2
    d = lax.axis_index("tm")
    s = lax.axis_index("space")
    has_before = d > 0
    has_after = d < n - 1

    small = [
        pltpu.make_async_copy(counts_hbm, counts, small_sem.at[0]),
        pltpu.make_async_copy(owner_hbm, owner, small_sem.at[1]),
        pltpu.make_async_copy(phase_hbm, phase, small_sem.at[2]),
        pltpu.make_async_copy(spread_hbm, spread, small_sem.at[3]),
        pltpu.make_async_copy(pick_hbm, pick, small_sem.at[4]),
    ]
    small[0].start()
    loads = {}
    for t in (1, 0):
        for k, size in enumerate(CHUNKS[t]):
            span = pl.ds(sum(CHUNKS[t][:k]), size)
            loads[t, k] = [
                pltpu.make_async_copy(
                    image_hbm.at[t, :, :, span], image.at[t, :, :, span], load_sem.at[0, t, k]
                ),
                pltpu.make_async_copy(
                    resid_hbm.at[t, :, span], resid.at[t, :, span], load_sem.at[1, t, k]
                ),
            ]
            if t == 1:
                loads[t, k].append(
                    pltpu.make_async_copy(
                        table_hbm.at[span], table.at[span], load_sem.at[2, t, k]
                    )
                )
            if t == 1 and k < EARLY:
                for copy in loads[t, k]:
                    copy.start()
            if t == 1 and k == 0:
                for copy in small[1:3]:
                    copy.start()

    barrier = pltpu.get_barrier_semaphore()

    def greet(where):
        pl.semaphore_signal(barrier, inc=1, device_id=where, device_id_type=MESH)

    greet((d, 1 - s))

    @pl.when(has_before)
    def _():
        greet((d - 1, 0))
        greet((d - 1, 1))

    @pl.when(has_after)
    def _():
        greet((d + 1, 0))
        greet((d + 1, 1))

    for copy in small[:3]:
        copy.wait()
    square = lax.broadcasted_iota(jnp.int32, (bricks, bricks), 0) == lax.broadcasted_iota(
        jnp.int32, (bricks, bricks), 1
    )

    def column(row):
        return jnp.sum(
            jnp.where(square, jnp.broadcast_to(row, (bricks, bricks)), 0.0), axis=1, keepdims=True
        )

    count = jnp.broadcast_to(column(counts[...].astype(F32)), (bricks, TILE))
    voxel = lax.broadcasted_iota(jnp.int32, (bricks, TILE), 1).astype(F32)
    lane = lax.broadcasted_iota(jnp.int32, (1, 128), 1)
    spare = lane % BLOCK >= MOMENTS

    def add_tiles(t, accs, begin, end):
        for tile in range(begin, end):
            unit, staging = tile % 2, tile // 2 % 2
            span = slice(tile * TILE, (tile + 1) * TILE)
            part = table[span, :]
            pltpu.matmul_push_rhs(jnp.concatenate([part, part], axis=1), staging, unit)
            if t == 1:
                mask[:, span] = jnp.where(voxel < count - tile * TILE, 1.0, 0.0).astype(BF16)
            valid = mask[:, span]
            g = [image[t, c, :, span] * valid for c in range(COMPS)]
            r = resid[t, :, span]
            products = [g[c] * g[e] for c, e in PAIRS] + [g[c] * r for c in range(COMPS)]
            for q, product in enumerate(products):
                pltpu.matmul_acc_lhs(accs[9 * unit + q], product, staging if q == 0 else None)

    def pop_sums(accs):
        return [
            (pltpu.matmul_pop(accs[q]) + pltpu.matmul_pop(accs[9 + q]))[:, :128] for q in range(9)
        ]

    def arranged(found):
        twos = []
        for c in range(COMPS):
            two = jnp.where(lane // BLOCK % 2 == 0, found[2 * c], found[2 * c + 1])
            two = jnp.where(spare, found[6 + c], two)
            twos.append(two + pltpu.roll(two, 64, 1))
        first = jnp.where(lane < 64, twos[0], twos[1])
        second = twos[2]
        return jnp.concatenate([first, second], axis=1)


    def slot_table():
        who = owner[...].astype(F32)
        who_column = column(who)
        earlier = lax.broadcasted_iota(jnp.int32, (bricks, bricks), 0) < lax.broadcasted_iota(
            jnp.int32, (bricks, bricks), 1
        )
        ones_before = jnp.sum(jnp.where(earlier, who_column, 0.0), axis=0, keepdims=True)
        place = lax.broadcasted_iota(jnp.int32, (1, bricks), 1).astype(F32)
        rank = jnp.where(who > 0.5, ones_before, place - ones_before)
        mine_first = jnp.where(s == 0, who, 1.0 - who)
        target = mine_first * cap + rank
        slot = lax.broadcasted_iota(jnp.int32, (2 * cap, bricks), 0).astype(F32)
        hit = jnp.where(slot == jnp.broadcast_to(target, (2 * cap, bricks)), 1.0, 0.0)
        hit = hit.astype(BF16)
        return jnp.concatenate([hit, hit, hit, jnp.zeros_like(hit)], axis=1)

    def start_place(x, hits, acc):
        pltpu.matmul_push_rhs(
            jnp.concatenate([*split3(x), jnp.zeros(x.shape, BF16)], axis=0), 0, 0
        )
        pltpu.matmul_acc_lhs(acc, hits, 0)

    def placed(acc):
        rows = pltpu.matmul_pop(acc)
        out = []
        for i in range(2):
            part = rows[i * cap : (i + 1) * cap]
            out.append(part[:, :128])
            out.append(jnp.where(lane < 64, part[:half, 128:], part[half:, 128:]))
        return jnp.concatenate(out, axis=0)

    first = jnp.where(has_before, 0.0, 1.0)
    last = jnp.where(has_after, 0.0, 1.0)

    def weights(t):
        u = phase[t]
        v = 1.0 - u
        return (
            v * v * v * (1.0 / 6.0),
            (3.0 * u * u * u - 6.0 * u * u + 4.0) * (1.0 / 6.0),
            (-3.0 * u * u * u + 3.0 * u * u + 3.0 * u + 1.0) * (1.0 / 6.0),
            u * u * u * (1.0 / 6.0),
        )

    w = weights(0)
    basis0 = (w[0] * (1.0 - first), w[1] + first * w[0], w[2] + last * w[3], w[3] * (1.0 - last))
    w = weights(1)
    basis1 = (w[0], w[1] + last * (w[2] + w[3]), w[2] * (1.0 - last), w[3] * (1.0 - last))
    size = cap + half

    def scale(b):
        return jnp.where(spare, b, b * b)

    def remote(src, dst, send_sem, recv_sem, where):
        return pltpu.make_async_remote_copy(
            src_ref=src,
            dst_ref=dst,
            send_sem=send_sem,
            recv_sem=recv_sem,
            device_id=where,
            device_id_type=MESH,
        )

    cores = (s, 1 - s)

    def to_after(k, i):
        return remote(
            send_fwd.at[k, i],
            recv_fwd.at[k, s],
            fwd_send_sem.at[k, i],
            fwd_recv_sem.at[k, s],
            (d + 1, cores[i]),
        )

    def to_before(i):
        return remote(
            send_back.at[i],
            recv_back.at[s],
            back_send_sem.at[i],
            back_recv_sem.at[s],
            (d - 1, cores[i]),
        )

    side = remote(send_side, mine.at[s], side_sem.at[0], side_sem.at[1], (d, 1 - s))

    def send_second(placed1):
        ahead = placed1 * scale(basis1[3])
        for i in range(2):
            send_fwd[1, i] = ahead[i * size : (i + 1) * size]

        pl.semaphore_wait(barrier, 1 + 2 * has_before.astype(jnp.int32) + 2 * has_after.astype(jnp.int32))

        @pl.when(jnp.logical_not(has_before))
        def _():
            recv_fwd[...] = jnp.zeros(recv_fwd.shape, F32)

        @pl.when(has_after)
        def _():
            for i in range(2):
                to_after(1, i).start()

        @pl.when(jnp.logical_not(has_after))
        def _():
            recv_back[...] = jnp.zeros(recv_back.shape, F32)

    tiles = voxels // TILE

    def second_step(*accs):
        done = 0
        for k, voxel_count in enumerate(CHUNKS[1]):
            for copy in loads[1, k]:
                copy.wait()
            if k == 0:
                for later in [(1, j) for j in range(EARLY, len(CHUNKS[1]))] + [(0, j) for j in range(len(CHUNKS[0]))]:
                    for copy in loads[later]:
                        copy.start()
                for copy in small[3:]:
                    copy.start()
            add_tiles(1, accs, done, done + voxel_count // TILE)
            done += voxel_count // TILE
            if k == 0:
                hits = slot_table()
        return hits, pop_sums(accs)

    def first_step(place_acc, *accs):
        for k in range(len(CHUNKS[0])):
            for copy in loads[0, k]:
                copy.wait()
        add_tiles(0, accs, 0, AHEAD)
        start_place(arranged(found), hits, place_acc)
        add_tiles(0, accs, AHEAD, 2 * AHEAD)
        placed1 = placed(place_acc)
        send_second(placed1)
        add_tiles(0, accs, 2 * AHEAD, tiles)
        start_place(arranged(pop_sums(accs)), hits, place_acc)
        return placed1, placed(place_acc)

    sums_acc = [pltpu.ACC(unit)((bricks, 256), F32) for unit in range(2) for _ in range(9)]
    hits, found = pl.run_scoped(second_step, *sums_acc)
    placed1, placed0 = pl.run_scoped(first_step, pltpu.ACC(0)((2 * cap, 256), F32), *sums_acc)
    ahead = placed0 * scale(basis0[3]) + placed1 * scale(basis1[2])
    for i in range(2):
        send_fwd[0, i] = ahead[i * size : (i + 1) * size]

    @pl.when(has_after)
    def _():
        for i in range(2):
            to_after(0, i).start()

    behind = placed0 * scale(basis0[0])
    for i in range(2):
        send_back[i] = behind[i * size : (i + 1) * size]

    @pl.when(has_before)
    def _():
        for i in range(2):
            to_before(i).start()

    for k in range(2):
        own = placed0 * scale(basis0[1 + k]) + placed1 * scale(basis1[k])
        mine[s, k] = own[:size]
        send_side[k] = own[size:]
    side.start()

    for copy in small[3:]:
        copy.wait()
    remote(send_side, mine.at[1 - s], side_sem.at[0], side_sem.at[1], (d, 1 - s)).wait_recv()

    @pl.when(has_after)
    def _():
        for i in range(2):
            remote(
                send_back.at[i],
                recv_back.at[i],
                back_send_sem.at[i],
                back_recv_sem.at[i],
                (d + 1, i),
            ).wait_recv()

    @pl.when(has_before)
    def _():
        for i in range(2):
            for k in range(2):
                remote(
                    send_fwd.at[k, i],
                    recv_fwd.at[k, i],
                    fwd_send_sem.at[k, i],
                    fwd_recv_sem.at[k, i],
                    (d - 1, i),
                ).wait_recv()

    for i in range(2):
        total_ref[0, i] = mine[i, 0] + recv_fwd[0, i]
        total_ref[1, i] = mine[i, 1] + recv_fwd[1, i] + recv_back[i]

    side.wait_send()

    @pl.when(has_after)
    def _():
        for i in range(2):
            to_after(1, i).wait_send()
            to_after(0, i).wait_send()

    @pl.when(has_before)
    def _():
        for i in range(2):
            to_before(i).wait_send()


def spread_kernel(total_ref, spread, pick, hess_hbm, grad_hbm, hess, grad, sem):
    cap = 2 * total_ref.shape[2] // 3
    half = cap // 2
    lane = lax.broadcasted_iota(jnp.int32, (1, 128), 1)
    copies = []

    def store(src, dst):
        copies.append(pltpu.make_async_copy(src, dst, sem.at[len(copies)]))
        copies[-1].start()

    for k in range(2):
        wide = []
        for i in range(2):
            tail = total_ref[k, i, cap:]
            for j in range(2):
                kept = jnp.where((lane < 64) == (j == 0), tail, 0.0)
                wide.append(
                    jnp.concatenate([total_ref[k, i, j * half : (j + 1) * half], kept], axis=1)
                )
        both = jnp.concatenate(split2(jnp.concatenate(wide, axis=0)), axis=0)
        slots = 2 * cap
        spread_both = jnp.dot(both, spread[...], preferred_element_type=F32)
        hess[k] = spread_both[:slots] + spread_both[slots:]
        store(hess.at[k], hess_hbm.at[k])
        grad[k] = dot_nt(pick[...], both[:slots]) + dot_nt(pick[...], both[slots:])
        store(grad.at[k], grad_hbm.at[k])
    for copy in copies:
        copy.wait()


def per_device(n, n_space, image_gradient, residual, phase, counts, owner):
    steps, bricks, comps, voxels = image_gradient.shape
    cap = 3 * bricks // (2 * n_space)
    slots = n_space * cap
    size = cap + cap // 2
    hessian_lanes, gradient_lanes = spread_tables()
    hbm = pl.BlockSpec(memory_space=pltpu.HBM)
    vmem = pl.BlockSpec(memory_space=pltpu.VMEM)
    chunks = max(map(len, CHUNKS))
    dma = pltpu.SemaphoreType.DMA
    totals, spread, pick = pl.pallas_call(
        functools.partial(kernel, n),
        out_shape=(
            jax.ShapeDtypeStruct((steps, 2, size, 128), F32),
            jax.ShapeDtypeStruct((256, PATCH), BF16),
            jax.ShapeDtypeStruct((DOFS, 256), BF16),
        ),
        in_specs=[hbm] * 8,
        out_specs=(vmem, vmem, vmem),
        scratch_shapes=[
            pltpu.VMEM((steps, comps, bricks, voxels), BF16),
            pltpu.VMEM((steps, bricks, voxels), BF16),
            pltpu.SMEM((steps,), F32),
            pltpu.VMEM((1, bricks), jnp.int32),
            pltpu.VMEM((1, bricks), jnp.int32),
            pltpu.VMEM((voxels, 128), BF16),
            pltpu.VMEM((bricks, voxels), BF16),
            pltpu.VMEM((2, 2, size, 128), F32),
            pltpu.VMEM((2, size, 128), F32),
            pltpu.VMEM((2, size, 128), F32),
            pltpu.VMEM((2, 2, size, 128), F32),
            pltpu.VMEM((2, size, 128), F32),
            pltpu.VMEM((2, 2, size, 128), F32),
            dma((3, 2, chunks)),
            dma((5,)),
            dma((2, 2)),
            dma((2, 2)),
            dma((2,)),
            dma((2,)),
            dma((2,)),
        ],
        compiler_params=pltpu.CompilerParams(
            collective_id=0, has_side_effects=True, vmem_limit_bytes=40 << 20
        ),
    )(
        *[
            pltpu.with_memory_space_constraint(x, pltpu.HBM)
            for x in (
                jnp.transpose(image_gradient, (0, 2, 1, 3)),
                residual,
                phase,
                counts.reshape(1, bricks),
                owner.reshape(1, bricks),
                jnp.asarray(moment_table()),
                jnp.asarray(hessian_lanes),
                jnp.asarray(gradient_lanes),
            )
        ]
    )
    hess, grad = pl.pallas_call(
        spread_kernel,
        out_shape=(
            jax.ShapeDtypeStruct((steps, slots, PATCH), F32),
            jax.ShapeDtypeStruct((steps, DOFS, slots), F32),
        ),
        in_specs=[vmem] * 3,
        out_specs=(hbm, hbm),
        scratch_shapes=[
            pltpu.VMEM((steps, slots, PATCH), F32),
            pltpu.VMEM((steps, DOFS, slots), F32),
            dma((2 * steps,)),
        ],
        compiler_params=pltpu.CompilerParams(vmem_limit_bytes=16 << 20),
    )(totals, spread, pick)
    return hess, jnp.transpose(grad, (0, 2, 1))


def solution(mesh):
    in_specs = (
        P("tm", "space", None, None),
        P("tm", "space", None),
        P("tm"),
        P("space"),
        P("space", None),
    )
    out_specs = (P("tm", "space", None), P("tm", "space", None))
    return jax.shard_map(
        functools.partial(per_device, mesh.shape["tm"], mesh.shape["space"]),
        mesh=mesh,
        in_specs=in_specs,
        out_specs=out_specs,
        check_vma=False,
    )
```
